32 devices in a mesh: bricks: 8 (over z, y), group: 4 (over x, core).
Axes of the slice: x: 2, y: 2, z: 4, core: 2. Of those that a mesh axis runs over, the one named last changes fastest.
Arguments:
- right_side: float32 [3, 128, 64, 128], P(None, 'bricks', 'group'), may hold values from -6 to 6
- material: int32 [128, 64, 128], P('bricks', 'group'), may hold values from 0 to 3
- brick_level: int32 [8, 4], P('bricks', 'group'), may hold values from 0 to 2
- mortar_rows: int32 [8, 4, 16], P('bricks', 'group'), may hold values from 0 to 15, each once within a row
- material_mu: float32 [4], replicated, may hold values from 0.5 to 4
- material_lam: float32 [4], replicated, may hold values from 0.25 to 2
- coarse_inverse: float32 [8, 48, 48], P('bricks'), may hold values from -1 to 5, as said below
Outputs:
- solution: float32 [3, 128, 64, 128], P(None, 'bricks', 'group')
- residual: float32 [3, 128, 64, 128], P(None, 'bricks', 'group')
The draws below stay inside these ranges and needn't reach their ends.
Inputs may be any that keep to these rules, and one draw needn't show every extreme that they name: `coarse_inverse`: each brick row's matrix is of full rank with a positive diagonal.
All inputs are finite; a program needn't handle non-finite values.
Results may differ from the reference program's by a relative error of at most 0.00027.
Values sent between devices are 32-bit elements; how exact they have to be, the bound alone decides.
A program may use at most 64 MiB of HBM per device.

```python
import math
import jax
import jax.numpy as jnp
from jax import lax

BX = 16
BY = 16
BZ = 128
BLOCK_XY = 16
BLOCK_Z = 32
CHEB = 4
NX = 128
NY = 64
CG = 48
N_BRICKS = 8
N_GROUP = 4


def draw_coarse_inverse(key, part):
    noise_key, diagonal_key = jax.random.split(jax.random.fold_in(key, 11))
    spread = 0.5 * jax.random.truncated_normal(noise_key, -4.0, 4.0, (N_BRICKS, CG, CG), jnp.float32)
    noise_part = spread / CG ** 0.5
    diagonal = jax.random.uniform(diagonal_key, (N_BRICKS, CG), jnp.float32, 2.0, 4.0)
    identity = (lax.broadcasted_iota(jnp.int32, (CG, CG), 0) == lax.broadcasted_iota(jnp.int32, (CG, CG), 1)).astype(jnp.float32)
    return noise_part + diagonal[:, :, None] * identity[None]


def plant(values, rng, low, top_value):
    longest = values.shape.index(max(values.shape))
    spots = []
    for shift in (0, 1):
        where = [jax.random.randint(jax.random.fold_in(rng, axis), (), 0, length) for axis, length in enumerate(values.shape)]
        where[longest] = (where[longest] + shift) % values.shape[longest]
        spots.append(tuple(where))
    return values.at[spots[0]].set(low).at[spots[1]].set(top_value)


def levels(own_key, shape, pieces, low, high):
    factor_of = 1.0
    for position, shards_of in pieces:
        steps = jax.random.uniform(jax.random.fold_in(jax.random.fold_in(own_key, 6), position), (shards_of,), jnp.float32, low / len(pieces), high / len(pieces))
        factor_of = factor_of * jnp.repeat(jnp.exp(steps), shape[position] // shards_of).reshape((-1,) + (1,) * (len(shape) - 1 - position))
    return factor_of


def noise(own_key, shape, scale, reach, cuts=(), kind=jnp.bfloat16):
    factor_of = levels(own_key, shape, cuts, -0.22, 0.18) if cuts else 1.0
    array = jax.random.normal(own_key, shape, jnp.float32) * scale * factor_of
    return jnp.minimum(jnp.maximum(array, -reach), reach).astype(kind)


def setup_inputs(seed: int = 0) -> dict:
    streams_of = jax.random.split(jax.random.key(seed), 8)
    right_side = noise(streams_of[0], (3, NX, NY, BZ), 1.0, 6.0, ((1, 8), (2, 4)), jnp.float32)
    material = plant(jax.random.randint(streams_of[1], (NX, NY, BZ), 0, 4), jax.random.fold_in(streams_of[1], 1), 0, 3).astype(jnp.int32)
    brick_level = plant(jax.random.randint(streams_of[2], (N_BRICKS, N_GROUP), 0, 3), jax.random.fold_in(streams_of[2], 1), 0, 2).astype(jnp.int32)
    mortar_rows = jax.vmap(lambda own: jax.random.permutation(own, BY))(jax.random.split(streams_of[3], N_BRICKS * N_GROUP)).reshape((N_BRICKS, N_GROUP, BY)).astype(jnp.int32)
    material_mu = jnp.clip(jnp.exp(jax.random.uniform(streams_of[4], (4,), jnp.float32, math.log(0.5), math.log(4.0))), 0.5, 4.0)
    material_lam = jnp.clip(jnp.exp(jax.random.uniform(streams_of[5], (4,), jnp.float32, math.log(0.25), math.log(2.0))), 0.25, 2.0)
    coarse_inverse = draw_coarse_inverse(jax.random.fold_in(streams_of[7], 71), 0)
    return dict(right_side=right_side, material=material, brick_level=brick_level, mortar_rows=mortar_rows, material_mu=material_mu, material_lam=material_lam, coarse_inverse=coarse_inverse)


low_ratio = 0.15
bound_margin = 1.1


def lookup(ids, table):
    total = jnp.zeros(ids.shape, table.dtype)
    for entry in range(4):
        total = total + jnp.where(ids == entry, table[entry], 0.0)
    return total


def neighbours(field, order, undo):
    count = field.shape[0]
    blocks = field.reshape(count, N_BRICKS, BX, N_GROUP, BY, BZ)
    last_face = blocks[:, :, BX - 1]
    first_face = blocks[:, :, 0]
    sent = jnp.take_along_axis(last_face, jnp.broadcast_to(order[None, :, :, :, None], last_face.shape), axis=3)
    below = jnp.concatenate([jnp.zeros_like(sent[:, :1]), sent[:, :-1]], axis=1)
    upper_faces = jnp.concatenate([first_face[:, 1:], jnp.zeros_like(first_face[:, :1])], axis=1)
    above = jnp.take_along_axis(upper_faces, jnp.broadcast_to(undo[None, :, :, :, None], upper_faces.shape), axis=3)
    x_plus = jnp.concatenate([blocks[:, :, 1:], above[:, :, None]], axis=2).reshape(field.shape)
    x_minus = jnp.concatenate([below[:, :, None], blocks[:, :, :-1]], axis=2).reshape(field.shape)
    y_plus = jnp.pad(field[:, :, 1:], ((0, 0), (0, 0), (0, 1), (0, 0)))
    y_minus = jnp.pad(field[:, :, :-1], ((0, 0), (0, 0), (1, 0), (0, 0)))
    z_plus = jnp.pad(field[:, :, :, 1:], ((0, 0), (0, 0), (0, 0), (0, 1)))
    z_minus = jnp.pad(field[:, :, :, :-1], ((0, 0), (0, 0), (0, 0), (1, 0)))
    return [x_plus, x_minus, y_plus, y_minus, z_plus, z_minus]


def chebyshev(solution, residual, apply, diagonal, lower, upper):
    theta = 0.5 * (upper + lower)
    delta = 0.5 * (upper - lower)
    sigma = theta / delta
    damping = 1.0 / sigma
    update = residual / (diagonal * theta)
    for turn in range(CHEB):
        solution = solution + update
        residual = residual - apply(update)
        if turn + 1 < CHEB:
            damping_next = 1.0 / (2.0 * sigma - damping)
            update = damping_next * damping * update + (2.0 * damping_next / delta) * (residual / diagonal)
            damping = damping_next
    return solution, residual


def reference(right_side, material, brick_level, mortar_rows, material_mu, material_lam, coarse_inverse):
    order = mortar_rows
    undo = jnp.argsort(mortar_rows, axis=-1).astype(jnp.int32)
    level_scale = jnp.exp2(2.0 * brick_level.astype(right_side.dtype))
    cell_scale = jnp.repeat(jnp.repeat(level_scale, BX, axis=0), BY, axis=1)[:, :, None]
    shear = lookup(material, material_mu) * cell_scale
    bulk = lookup(material, material_lam) * cell_scale
    x_index = lax.broadcasted_iota(jnp.int32, (NX, NY, BZ), 0)
    y_index = lax.broadcasted_iota(jnp.int32, (NX, NY, BZ), 1)
    z_index = lax.broadcasted_iota(jnp.int32, (NX, NY, BZ), 2)
    outside = [x_index == NX - 1, x_index == 0, y_index == NY - 1, y_index == 0, z_index == BZ - 1, z_index == 0]
    shear_near = neighbours(shear[None], order, undo)
    weights = [jnp.where(edge, shear, 0.5 * (shear + other[0])) for edge, other in zip(outside, shear_near)]
    weight_total = weights[0]
    for extra in weights[1:]:
        weight_total = weight_total + extra
    diagonal = weight_total + 1.5 * bulk
    bound_ratio = (2.0 * weight_total + 2.5 * bulk) / diagonal
    upper = bound_margin * jnp.max(bound_ratio)
    lower = low_ratio * upper

    def apply(field):
        near = neighbours(field, order, undo)
        coupled = jnp.sum(field, axis=0)
        result = weight_total * field + bulk * (field + 0.5 * coupled)
        for weight, value in zip(weights, near):
            result = result - weight * value
        return result

    solution = jnp.zeros_like(right_side)
    solution, residual = chebyshev(solution, right_side, apply, diagonal, lower, upper)
    cells_x = BX // BLOCK_XY
    cells_y = BY // BLOCK_XY
    cells_z = BZ // BLOCK_Z
    shaped = residual.reshape(3, N_BRICKS, cells_x, BLOCK_XY, N_GROUP, cells_y, BLOCK_XY, cells_z, BLOCK_Z)
    coarse = jnp.mean(shaped, axis=(3, 6, 8))
    coarse = coarse.transpose(1, 3, 0, 2, 4, 5).reshape(N_BRICKS, CG)
    correction = jnp.einsum('bij,bj->bi', coarse_inverse, coarse, precision=lax.Precision.HIGHEST)
    spread = correction.reshape(N_BRICKS, N_GROUP, 3, cells_x, cells_y, cells_z).transpose(2, 0, 3, 1, 4, 5)
    fine = jnp.broadcast_to(spread[:, :, :, None, :, :, None, :, None], (3, N_BRICKS, cells_x, BLOCK_XY, N_GROUP, cells_y, BLOCK_XY, cells_z, BLOCK_Z)).reshape(3, NX, NY, BZ)
    solution = solution + fine
    residual = residual - apply(fine)
    solution, residual = chebyshev(solution, residual, apply, diagonal, lower, upper)
    return solution, residual
```

```python
import functools

import jax
import jax.numpy as jnp
from jax import lax
from jax.experimental import pallas as pl
from jax.experimental.pallas import tpu as pltpu
from jax.sharding import PartitionSpec as P

BLOCK_Z = 32
CHEB = 4
LOW_RATIO = 0.15
BOUND_MARGIN = 1.1
ROUNDS = 2 * CHEB
UNROLL = 4
HIGHEST = lax.Precision.HIGHEST


def kernel(
    nb, ng, dx, dy, dz,
    rhs, material, level, mortar, mu, lam, inverse,
    sol, res,
    u, r, shear, wx, wyp, wym, wzp, wzm, dg, hb, invd, coef, undo,
    s_send_up, s_send_y, s_recv, above, up_send, y_send, recv,
    m_own, m_all, m2_own, m2_all, c_own, c_all, f_all, fx_own, fx_recv,
    s_ssem, s_rsem, h_ssem, h_rsem,
    m_ssem, m_rsem, m2_ssem, m2_rsem, c_ssem, c_rsem, f_ssem, f_rsem,
):
    b = lax.axis_index("bricks")
    g = lax.axis_index("group")
    has = [b > 0, b < nb - 1, g > 0, g < ng - 1]
    sends = [has[1], has[0], has[3], has[2]]
    peers = [(b + 1, g), (b - 1, g), (b, g + 1), (b, g - 1)]

    def remote(src, dst, ssem, rsem, peer):
        return pltpu.make_async_remote_copy(
            src_ref=src, dst_ref=dst, send_sem=ssem, recv_sem=rsem,
            device_id=peer, device_id_type=pl.DeviceIdType.MESH,
        )

    barrier = pltpu.get_barrier_semaphore()
    others = [(b, lax.rem(g + k, ng)) for k in range(1, ng)]
    others += [(lax.rem(b + k, nb), g) for k in range(1, nb)]
    for peer in others:
        pl.semaphore_signal(
            barrier, inc=1, device_id=peer, device_id_type=pl.DeviceIdType.MESH
        )

    scale = jnp.where(level[0, 0] == 0, 1.0, jnp.where(level[0, 0] == 1, 4.0, 16.0))
    zero_face = jnp.zeros((3, dx, dz), jnp.float32)

    order = [mortar[0, 0, k] for k in range(dy)]
    for k in range(dy):
        total = jnp.int32(0)
        for j in range(dy):
            total = jnp.where(order[j] == k, jnp.int32(j), total)
        undo[k] = total

    def lookup(ids, table):
        total = jnp.where(ids == 0, table[0] * scale, 0.0)
        for entry in range(1, 4):
            total = jnp.where(ids == entry, table[entry] * scale, total)
        return total

    def shear_plane(i, _):
        ids = material[i]
        plane = lookup(ids, mu)
        shear[i + 1] = plane
        hb[i] = lookup(ids, lam)
        s_send_y[0, pl.ds(i, 1), :] = plane[dy - 1 : dy]
        s_send_y[1, pl.ds(i, 1), :] = plane[0:1]
        return 0

    lax.fori_loop(0, dx, shear_plane, 0, unroll=UNROLL)
    for k in range(dy):
        s_send_up[k : k + 1, :] = shear[dx, pl.ds(order[k], 1), :]

    pl.semaphore_wait(barrier, len(others))

    def s_copy(d):
        src = [s_send_up, shear.at[1], s_send_y.at[0], s_send_y.at[1]][d]
        return remote(src, s_recv.at[d], s_ssem.at[d], s_rsem.at[d], peers[d])

    def exchange_start(copy):
        for d in range(4):
            @pl.when(sends[d])
            def _():
                copy(d).start()

    def exchange_wait(copy):
        for d in range(4):
            @pl.when(has[d])
            def _():
                copy(d).wait_recv()
        for d in range(4):
            @pl.when(sends[d])
            def _():
                copy(d).wait_send()

    exchange_start(s_copy)

    @pl.when(b == 0)
    def _():
        s_recv[0] = shear[1]

    @pl.when(b == nb - 1)
    def _():
        shear[dx + 1] = shear[dx]

    @pl.when(g == 0)
    def _():
        s_recv[2] = s_send_y[1]

    @pl.when(g == ng - 1)
    def _():
        s_recv[3] = s_send_y[0]

    for d in range(4):
        @pl.when(jnp.logical_not(has[d]))
        def _():
            for turn in range(ROUNDS):
                recv[turn, d] = zero_face
            if d < 2:
                fx_recv[d] = jnp.zeros(fx_recv.shape[1:], jnp.float32)

    exchange_wait(s_copy)
    shear[0] = s_recv[0]

    @pl.when(b < nb - 1)
    def _():
        for k in range(dy):
            shear[dx + 1, k : k + 1, :] = s_recv[1, pl.ds(undo[k], 1), :]

    row = lax.broadcasted_iota(jnp.int32, (dy, dz), 0)
    lane = lax.broadcasted_iota(jnp.int32, (dy, dz), 1)

    def y_near(v, low, high):
        ym = jnp.where(row == 0, jnp.broadcast_to(low, v.shape), pltpu.roll(v, 1, 0))
        yp = jnp.where(
            row == dy - 1, jnp.broadcast_to(high, v.shape), pltpu.roll(v, dy - 1, 0)
        )
        return ym, yp

    def z_near(v):
        return pltpu.roll(v, 1, 1), pltpu.roll(v, dz - 1, 1)

    wx[0] = 0.5 * (shear[0] + shear[1])

    def weight_plane(i, best):
        s = shear[i + 1]
        xp = 0.5 * (s + shear[i + 2])
        wx[i + 1] = xp
        xm = 0.5 * (s + shear[i])
        ym, yp = y_near(s, s_recv[2, pl.ds(i, 1), :], s_recv[3, pl.ds(i, 1), :])
        ym = 0.5 * (s + ym)
        yp = 0.5 * (s + yp)
        zm, zp = z_near(s)
        zm = 0.5 * (s + zm)
        zp = 0.5 * (s + zp)
        wyp[i] = yp
        wym[i] = ym
        wzp[i] = jnp.where(lane == dz - 1, 0.0, zp)
        wzm[i] = jnp.where(lane == 0, 0.0, zm)
        total = xp + xm + yp + ym + jnp.where(lane == dz - 1, s, zp) + jnp.where(lane == 0, s, zm)
        bulk = hb[i]
        diagonal = total + 1.5 * bulk
        inv = 1.0 / diagonal
        invd[i] = inv
        dg[i] = total + bulk
        hb[i] = 0.5 * bulk
        for c in range(3):
            d0 = rhs[c, i] * inv
            u[0, c, i + 1] = d0
            y_send[0, 0, c, pl.ds(i, 1), :] = d0[dy - 1 : dy]
            y_send[0, 1, c, pl.ds(i, 1), :] = d0[0:1]
        return jnp.maximum(best, (2.0 * total + 2.5 * bulk) / diagonal)

    best = lax.fori_loop(0, dx, weight_plane, jnp.zeros((dy, dz), jnp.float32), unroll=2)
    m_own[...] = jnp.broadcast_to(jnp.max(best, axis=0, keepdims=True), m_own.shape)

    def h_copy(turn, slot):
        def copy(d):
            src = [
                up_send.at[turn], u.at[slot, :, 1], y_send.at[turn, 0], y_send.at[turn, 1]
            ][d]
            return remote(
                src, recv.at[turn, d], h_ssem.at[turn, d], h_rsem.at[turn, d], peers[d]
            )
        return copy

    def halo_start(turn, slot):
        for c in range(3):
            for k in range(dy):
                up_send[turn, c, k : k + 1, :] = u[slot, c, dx, pl.ds(order[k], 1), :]
        exchange_start(h_copy(turn, slot))

    def halo_wait(turn, slot):
        exchange_wait(h_copy(turn, slot))
        for c in range(3):
            u[slot, c, 0] = recv[turn, 0, c]
            above[c] = recv[turn, 1, c]
        for c in range(3):
            for k in range(dy):
                u[slot, c, dx + 1, k : k + 1, :] = above[c, pl.ds(undo[k], 1), :]

    def apply_plane(i, slot, low, high):
        v = [u[slot, c, i + 1] for c in range(3)]
        coupled = hb[i] * (v[0] + v[1] + v[2])
        out = []
        for c in range(3):
            ym, yp = y_near(v[c], low(c, i), high(c, i))
            zm, zp = z_near(v[c])
            near = wx[i] * u[slot, c, i] + wx[i + 1] * u[slot, c, i + 2]
            near = near + wym[i] * ym + wyp[i] * yp + wzm[i] * zm + wzp[i] * zp
            out.append(dg[i] * v[c] + coupled - near)
        return v, out

    def recv_rows(turn):
        return (
            lambda c, i: recv[turn, 2, c, pl.ds(i, 1), :],
            lambda c, i: recv[turn, 3, c, pl.ds(i, 1), :],
        )

    def bcoef(k):
        return jnp.broadcast_to(coef[k : k + 1, :], (dy, dz))

    def ring_start(own, store, ssem, rsem, peer_of, count, mine):
        copies = []
        for k in range(1, count):
            copies.append(remote(own, store.at[k], ssem.at[k], rsem.at[k], peer_of(k)))
        for copy in copies:
            copy.start()
        return copies

    group_peer = lambda k: (b, lax.rem(g + k, ng))
    brick_peer = lambda k: (lax.rem(b + k, nb), g)

    halo_start(0, 0)
    m_copies = ring_start(m_own, m_all, m_ssem, m_rsem, group_peer, ng, g)
    halo_wait(0, 0)

    low, high = recv_rows(0)

    def first_plane(i, _):
        _, out = apply_plane(i, 0, low, high)
        inv = invd[i]
        for c in range(3):
            r[c, i] = out[c]
            q = out[c] * inv
            u[1, c, i + 1] = q
            y_send[1, 0, c, pl.ds(i, 1), :] = q[dy - 1 : dy]
            y_send[1, 1, c, pl.ds(i, 1), :] = q[0:1]
        return 0

    lax.fori_loop(0, dx, first_plane, 0, unroll=UNROLL)
    halo_start(1, 1)
    top = m_own[...]
    for k, copy in enumerate(m_copies):
        copy.wait()
        top = jnp.maximum(top, m_all[k + 1])
    m2_own[...] = top
    m2_copies = ring_start(m2_own, m2_all, m2_ssem, m2_rsem, brick_peer, nb, b)
    halo_wait(1, 1)
    for k, copy in enumerate(m2_copies):
        copy.wait()
        top = jnp.maximum(top, m2_all[k + 1])
    upper = BOUND_MARGIN * jnp.broadcast_to(jnp.max(top, axis=1, keepdims=True), top.shape)
    lower = LOW_RATIO * upper
    theta = 0.5 * (upper + lower)
    delta = 0.5 * (upper - lower)
    sigma = theta / delta
    damping = 1.0 / sigma
    inv_theta = 1.0 / theta
    coef[0:8] = inv_theta
    rows = []
    for turn in range(1, CHEB):
        following = 1.0 / (2.0 * sigma - damping)
        rows.append((following * damping, 2.0 * following / delta))
        damping = following
    for turn, (a, c2) in enumerate(rows):
        coef[8 + 2 * turn : 9 + 2 * turn] = a[0:1]
        coef[9 + 2 * turn : 10 + 2 * turn] = c2[0:1]
    coef[14:15] = (rows[0][0] * inv_theta + rows[0][1])[0:1]
    coef[15:16] = (rows[0][1] * inv_theta)[0:1]

    alpha, beta, it = bcoef(14), bcoef(15), bcoef(0)

    def combine_plane(i, _):
        for c in range(3):
            d0 = u[0, c, i + 1]
            sol[c, i] = d0 * it
            res[c, i] = rhs[c, i] - r[c, i] * it
            u[0, c, i + 1] = alpha * d0 - beta * u[1, c, i + 1]
        return 0

    lax.fori_loop(0, dx, combine_plane, 0, unroll=UNROLL)
    for c in range(3):
        for p in (0, dx + 1):
            u[0, c, p] = alpha * u[0, c, p] - beta * u[1, c, p]
        for d in (2, 3):
            recv[1, d, c] = alpha[:dx] * recv[0, d, c] - beta[:dx] * recv[1, d, c]

    def step(slot, low, high, a, c2, following):
        other = 1 - slot

        def plane(i, sums):
            v, out = apply_plane(i, slot, low, high)
            inv = invd[i]
            new = []
            for c in range(3):
                rest = res[c, i] - out[c]
                res[c, i] = rest
                sol[c, i] = sol[c, i] + v[c]
                if following is None:
                    new.append(sums[c] + rest)
                    continue
                ahead = c2 * (rest * inv)
                if a is not None:
                    ahead = ahead + a * v[c]
                u[other, c, i + 1] = ahead
                y_send[following, 0, c, pl.ds(i, 1), :] = ahead[dy - 1 : dy]
                y_send[following, 1, c, pl.ds(i, 1), :] = ahead[0:1]
            return tuple(new)

        init = ()
        if following is None:
            init = tuple(jnp.zeros((dy, dz), jnp.float32) for _ in range(3))
        return lax.fori_loop(0, dx, plane, init, unroll=UNROLL)

    slot = 0
    for turn in range(1, CHEB):
        low, high = recv_rows(turn)
        if turn + 1 < CHEB:
            step(slot, low, high, bcoef(8 + 2 * turn), bcoef(9 + 2 * turn), turn + 1)
            slot = 1 - slot
            halo_start(turn + 1, slot)
            halo_wait(turn + 1, slot)
        else:
            sums = step(slot, low, high, None, None, None)

    c_own[...] = jnp.zeros(c_own.shape, jnp.float32)
    for c in range(3):
        c_own[c : c + 1, :] = jnp.sum(sums[c], axis=0, keepdims=True)
    c_all[g] = c_own[...]
    c_copies = [
        remote(c_own, c_all.at[g], c_ssem.at[k], c_rsem.at[k], group_peer(k))
        for k in range(1, ng)
    ]
    for copy in c_copies:
        copy.start()
    for k in range(1, ng):
        source = lax.rem(g + ng - k, ng)
        remote(c_own, c_all.at[source], c_ssem.at[k], c_rsem.at[k], group_peer(k)).wait()
    cells_z = dz // BLOCK_Z
    size = 3 * cells_z * ng
    flat = c_all[...].reshape(ng * 8, dz)
    li = lax.broadcasted_iota(jnp.int32, (dz, size), 0)
    ki = lax.broadcasted_iota(jnp.int32, (dz, size), 1)
    gather = jnp.where(li // BLOCK_Z == ki % cells_z, 1.0 / (dx * dy * BLOCK_Z), 0.0)
    spread = jnp.dot(flat, gather, precision=HIGHEST, preferred_element_type=jnp.float32)
    ri = lax.broadcasted_iota(jnp.int32, (ng * 8, size), 0)
    kk = lax.broadcasted_iota(jnp.int32, (ng * 8, size), 1) // cells_z
    mine = (ri // 8 == kk // 3) & (ri % 8 == kk % 3)
    vector = jnp.sum(jnp.where(mine, spread, 0.0), axis=0, keepdims=True)
    correction = jnp.sum(inverse[0] * vector, axis=1, keepdims=True)
    bi = lax.broadcasted_iota(jnp.int32, (size, dz), 0)
    bl = lax.broadcasted_iota(jnp.int32, (size, dz), 1)
    table = jnp.where(bi % cells_z == bl // BLOCK_Z, jnp.broadcast_to(correction, (size, dz)), 0.0)
    f_all[...] = jnp.zeros(f_all.shape, jnp.float32)
    for k in range(ng):
        for c in range(3):
            start = (k * 3 + c) * cells_z
            f_all[k + 1, c : c + 1, :] = jnp.sum(
                table[start : start + cells_z], axis=0, keepdims=True
            )
    fx_own[...] = f_all[g + 1]

    def f_copy(d):
        return remote(fx_own, fx_recv.at[d], f_ssem.at[d], f_rsem.at[d], peers[d])

    for d in range(2):
        @pl.when(sends[d])
        def _():
            f_copy(d).start()

    slot = 0

    def fill_plane(i, _):
        for c in range(3):
            u[0, c, i + 1] = jnp.broadcast_to(fx_own[c : c + 1, :], (dy, dz))
        return 0

    lax.fori_loop(0, dx, fill_plane, 0, unroll=UNROLL)
    for d in range(2):
        @pl.when(has[d])
        def _():
            f_copy(d).wait_recv()
        @pl.when(sends[d])
        def _():
            f_copy(d).wait_send()
    for c in range(3):
        u[0, c, 0] = jnp.broadcast_to(fx_recv[0, c : c + 1, :], (dy, dz))
        u[0, c, dx + 1] = jnp.broadcast_to(fx_recv[1, c : c + 1, :], (dy, dz))
    step(
        0,
        lambda c, i: f_all[g, c : c + 1, :],
        lambda c, i: f_all[g + 2, c : c + 1, :],
        None,
        bcoef(0),
        CHEB,
    )
    slot = 1
    for turn in range(CHEB):
        halo_start(CHEB + turn, slot)
        halo_wait(CHEB + turn, slot)
        low, high = recv_rows(CHEB + turn)
        if turn + 1 < CHEB:
            step(slot, low, high, bcoef(8 + 2 * turn), bcoef(9 + 2 * turn), CHEB + turn + 1)
            slot = 1 - slot
        else:
            step(slot, low, high, None, None, None)


def per_device(rhs, material, level, mortar, mu, lam, inverse):
    nb = lax.axis_size("bricks")
    ng = lax.axis_size("group")
    dx, dy, dz = material.shape
    f32 = jnp.float32
    vmem = pl.BlockSpec(memory_space=pltpu.VMEM)
    smem = pl.BlockSpec(memory_space=pltpu.SMEM)
    dma = pltpu.SemaphoreType.DMA
    grid = pltpu.VMEM((dx, dy, dz), f32)
    scratch = [
        pltpu.VMEM((2, 3, dx + 2, dy, dz), f32),
        pltpu.VMEM((3, dx, dy, dz), f32),
        pltpu.VMEM((dx + 2, dy, dz), f32),
        pltpu.VMEM((dx + 1, dy, dz), f32),
        grid, grid, grid, grid, grid, grid, grid,
        pltpu.VMEM((16, dz), f32),
        pltpu.SMEM((dy,), jnp.int32),
        pltpu.VMEM((dy, dz), f32),
        pltpu.VMEM((2, dx, dz), f32),
        pltpu.VMEM((4, dx, dz), f32),
        pltpu.VMEM((3, dy, dz), f32),
        pltpu.VMEM((ROUNDS, 3, dy, dz), f32),
        pltpu.VMEM((ROUNDS, 2, 3, dx, dz), f32),
        pltpu.VMEM((ROUNDS, 4, 3, dx, dz), f32),
        pltpu.VMEM((8, dz), f32),
        pltpu.VMEM((ng, 8, dz), f32),
        pltpu.VMEM((8, dz), f32),
        pltpu.VMEM((nb, 8, dz), f32),
        pltpu.VMEM((8, dz), f32),
        pltpu.VMEM((ng, 8, dz), f32),
        pltpu.VMEM((ng + 2, 8, dz), f32),
        pltpu.VMEM((8, dz), f32),
        pltpu.VMEM((2, 8, dz), f32),
        dma((4,)), dma((4,)),
        dma((ROUNDS, 4)), dma((ROUNDS, 4)),
        dma((ng,)), dma((ng,)),
        dma((nb,)), dma((nb,)),
        dma((ng,)), dma((ng,)),
        dma((2,)), dma((2,)),
    ]
    return pl.pallas_call(
        functools.partial(kernel, nb, ng, dx, dy, dz),
        out_shape=(
            jax.ShapeDtypeStruct(rhs.shape, f32),
            jax.ShapeDtypeStruct(rhs.shape, f32),
        ),
        in_specs=[vmem, vmem, smem, smem, smem, smem, vmem],
        out_specs=(vmem, vmem),
        scratch_shapes=scratch,
        compiler_params=pltpu.CompilerParams(collective_id=0, has_side_effects=True),
    )(rhs, material, level, mortar, mu, lam, inverse)


def solution(mesh):
    return jax.shard_map(
        per_device,
        mesh=mesh,
        in_specs=(
            P(None, "bricks", "group", None),
            P("bricks", "group", None),
            P("bricks", "group"),
            P("bricks", "group", None),
            P(),
            P(),
            P("bricks", None, None),
        ),
        out_specs=(P(None, "bricks", "group", None), P(None, "bricks", "group", None)),
        check_vma=False,
    )
```

```python
import functools

import jax
import jax.numpy as jnp
from jax import lax
from jax.experimental import pallas as pl
from jax.experimental.pallas import tpu as pltpu
from jax.sharding import PartitionSpec as P

BLOCK_Z = 32
CHEB = 4
LOW_RATIO = 0.15
BOUND_MARGIN = 1.1
ROUNDS = 2 * CHEB
UNROLL = 4
SWEEP = 7
HIGHEST = lax.Precision.HIGHEST


def kernel(
    nb, ng, dx, dy, dz,
    rhs, material, level, mortar, mu, lam, inverse,
    sol, res,
    u, r, shear, wx, wyp, wym, wzp, wzm, dg, hb, invd, coef, undo,
    s_send_up, s_send_y, s_recv, above, up_send, y_send, recv,
    m_own, m_all, m2_own, m2_all, c_own, c_all, f_all, fx_own, fx_recv,
    s_ssem, s_rsem, h_ssem, h_rsem,
    m_ssem, m_rsem, m2_ssem, m2_rsem, c_ssem, c_rsem, f_ssem, f_rsem,
):
    b = lax.axis_index("bricks")
    g = lax.axis_index("group")
    has = [b > 0, b < nb - 1, g > 0, g < ng - 1]
    sends = [has[1], has[0], has[3], has[2]]
    peers = [(b + 1, g), (b - 1, g), (b, g + 1), (b, g - 1)]

    def remote(src, dst, ssem, rsem, peer):
        return pltpu.make_async_remote_copy(
            src_ref=src, dst_ref=dst, send_sem=ssem, recv_sem=rsem,
            device_id=peer, device_id_type=pl.DeviceIdType.MESH,
        )

    barrier = pltpu.get_barrier_semaphore()
    others = [(b, lax.rem(g + k, ng)) for k in range(1, ng)]
    others += [(lax.rem(b + k, nb), g) for k in range(1, nb)]
    for peer in others:
        pl.semaphore_signal(
            barrier, inc=1, device_id=peer, device_id_type=pl.DeviceIdType.MESH
        )

    grade = jnp.broadcast_to(level[...], (dy, dz))
    scale = jnp.where(grade == 0, 1.0, jnp.where(grade == 1, 4.0, 16.0))
    zero_face = jnp.zeros((3, dx, dz), jnp.float32)

    order = [mortar[0, 0, k] for k in range(dy)]
    for k in range(dy):
        total = jnp.int32(0)
        for j in range(dy):
            total = jnp.where(order[j] == k, jnp.int32(j), total)
        undo[k] = total

    def lookup(ids, table):
        total = jnp.where(ids == 0, table[0], 0.0)
        for entry in range(1, 4):
            total = jnp.where(ids == entry, table[entry], total)
        return total * scale

    def shear_plane(i, _):
        ids = material[i]
        plane = lookup(ids, mu)
        shear[i + 1] = plane
        hb[i] = lookup(ids, lam)
        s_send_y[0, pl.ds(i, 1), :] = plane[dy - 1 : dy]
        s_send_y[1, pl.ds(i, 1), :] = plane[0:1]
        return 0

    lax.fori_loop(0, dx, shear_plane, 0, unroll=UNROLL)
    for k in range(dy):
        s_send_up[k : k + 1, :] = shear[dx, pl.ds(order[k], 1), :]

    pl.semaphore_wait(barrier, len(others))

    def s_copy(d):
        src = [s_send_up, shear.at[1], s_send_y.at[0], s_send_y.at[1]][d]
        return remote(src, s_recv.at[d], s_ssem.at[d], s_rsem.at[d], peers[d])

    def exchange_start(copy, directions=(0, 1, 2, 3)):
        for d in directions:
            @pl.when(sends[d])
            def _():
                copy(d).start()

    def exchange_wait(copy):
        for d in range(4):
            @pl.when(has[d])
            def _():
                copy(d).wait_recv()
        for d in range(4):
            @pl.when(sends[d])
            def _():
                copy(d).wait_send()

    exchange_start(s_copy)

    @pl.when(b == 0)
    def _():
        s_recv[0] = shear[1]

    @pl.when(b == nb - 1)
    def _():
        shear[dx + 1] = shear[dx]

    @pl.when(g == 0)
    def _():
        s_recv[2] = s_send_y[1]

    @pl.when(g == ng - 1)
    def _():
        s_recv[3] = s_send_y[0]

    for d in range(4):
        @pl.when(jnp.logical_not(has[d]))
        def _():
            for turn in range(ROUNDS):
                recv[turn, d] = zero_face
            if d < 2:
                fx_recv[d] = jnp.zeros(fx_recv.shape[1:], jnp.float32)

    exchange_wait(s_copy)
    shear[0] = s_recv[0]

    @pl.when(b < nb - 1)
    def _():
        for k in range(dy):
            shear[dx + 1, k : k + 1, :] = s_recv[1, pl.ds(undo[k], 1), :]

    row = lax.broadcasted_iota(jnp.int32, (dy, dz), 0)
    lane = lax.broadcasted_iota(jnp.int32, (dy, dz), 1)

    def y_near(v, low, high):
        ym = jnp.where(row == 0, jnp.broadcast_to(low, v.shape), pltpu.roll(v, 1, 0))
        yp = jnp.where(
            row == dy - 1, jnp.broadcast_to(high, v.shape), pltpu.roll(v, dy - 1, 0)
        )
        return ym, yp

    def z_near(v):
        return pltpu.roll(v, 1, 1), pltpu.roll(v, dz - 1, 1)

    def h_copy(turn, slot):
        def copy(d):
            src = [
                up_send.at[turn], u.at[slot, :, 1], y_send.at[turn, 0], y_send.at[turn, 1]
            ][d]
            return remote(
                src, recv.at[turn, d], h_ssem.at[turn, d], h_rsem.at[turn, d], peers[d]
            )
        return copy

    def sweep(plane, turn, slot, carry, unroll):
        carry = plane(0, carry)
        carry = plane(dx - 1, carry)
        if turn is not None:
            for c in range(3):
                for k in range(dy):
                    up_send[turn, c, k : k + 1, :] = u[slot, c, dx, pl.ds(order[k], 1), :]
            exchange_start(h_copy(turn, slot), (0, 1))
        carry = lax.fori_loop(1, dx - 1, plane, carry, unroll=unroll)
        if turn is not None:
            exchange_start(h_copy(turn, slot), (2, 3))
        return carry

    wx[0] = 0.5 * (shear[0] + shear[1])
    wx[dx] = 0.5 * (shear[dx] + shear[dx + 1])

    def weight_plane(i, best):
        s = shear[i + 1]
        xp = 0.5 * (s + shear[i + 2])
        wx[i + 1] = xp
        xm = 0.5 * (s + shear[i])
        ym, yp = y_near(s, s_recv[2, pl.ds(i, 1), :], s_recv[3, pl.ds(i, 1), :])
        ym = 0.5 * (s + ym)
        yp = 0.5 * (s + yp)
        zm, zp = z_near(s)
        zm = 0.5 * (s + zm)
        zp = 0.5 * (s + zp)
        wyp[i] = yp
        wym[i] = ym
        wzp[i] = jnp.where(lane == dz - 1, 0.0, zp)
        wzm[i] = jnp.where(lane == 0, 0.0, zm)
        total = xp + xm + yp + ym + jnp.where(lane == dz - 1, s, zp) + jnp.where(lane == 0, s, zm)
        bulk = hb[i]
        diagonal = total + 1.5 * bulk
        inv = 1.0 / diagonal
        invd[i] = inv
        dg[i] = total + bulk
        hb[i] = 0.5 * bulk
        for c in range(3):
            d0 = rhs[c, i] * inv
            u[0, c, i + 1] = d0
            y_send[0, 0, c, pl.ds(i, 1), :] = d0[dy - 1 : dy]
            y_send[0, 1, c, pl.ds(i, 1), :] = d0[0:1]
        return jnp.maximum(best, (2.0 * total + 2.5 * bulk) / diagonal)

    best = sweep(weight_plane, 0, 0, jnp.zeros((dy, dz), jnp.float32), 2)
    m_own[...] = jnp.broadcast_to(jnp.max(best, axis=0, keepdims=True), m_own.shape)

    def halo_wait(turn, slot):
        exchange_wait(h_copy(turn, slot))
        for c in range(3):
            u[slot, c, 0] = recv[turn, 0, c]
            above[c] = recv[turn, 1, c]
        for c in range(3):
            for k in range(dy):
                u[slot, c, dx + 1, k : k + 1, :] = above[c, pl.ds(undo[k], 1), :]

    def apply_plane(i, slot, low, high):
        v = [u[slot, c, i + 1] for c in range(3)]
        coupled = hb[i] * (v[0] + v[1] + v[2])
        out = []
        for c in range(3):
            ym, yp = y_near(v[c], low(c, i), high(c, i))
            zm, zp = z_near(v[c])
            near = wx[i] * u[slot, c, i] + wx[i + 1] * u[slot, c, i + 2]
            near = near + wym[i] * ym + wyp[i] * yp + wzm[i] * zm + wzp[i] * zp
            out.append(dg[i] * v[c] + coupled - near)
        return v, out

    def recv_rows(turn):
        return (
            lambda c, i: recv[turn, 2, c, pl.ds(i, 1), :],
            lambda c, i: recv[turn, 3, c, pl.ds(i, 1), :],
        )

    def bcoef(k):
        return jnp.broadcast_to(coef[k : k + 1, :], (dy, dz))

    def ring_start(own, store, ssem, rsem, peer_of, count, mine):
        copies = []
        for k in range(1, count):
            copies.append(remote(own, store.at[k], ssem.at[k], rsem.at[k], peer_of(k)))
        for copy in copies:
            copy.start()
        return copies

    group_peer = lambda k: (b, lax.rem(g + k, ng))
    brick_peer = lambda k: (lax.rem(b + k, nb), g)

    m_copies = ring_start(m_own, m_all, m_ssem, m_rsem, group_peer, ng, g)
    halo_wait(0, 0)

    low, high = recv_rows(0)

    def first_plane(i, _):
        _, out = apply_plane(i, 0, low, high)
        inv = invd[i]
        for c in range(3):
            r[c, i] = out[c]
            q = out[c] * inv
            u[1, c, i + 1] = q
            y_send[1, 0, c, pl.ds(i, 1), :] = q[dy - 1 : dy]
            y_send[1, 1, c, pl.ds(i, 1), :] = q[0:1]
        return 0

    sweep(first_plane, 1, 1, 0, SWEEP)
    top = m_own[...]
    for k, copy in enumerate(m_copies):
        copy.wait()
        top = jnp.maximum(top, m_all[k + 1])
    m2_own[...] = top
    m2_copies = ring_start(m2_own, m2_all, m2_ssem, m2_rsem, brick_peer, nb, b)
    halo_wait(1, 1)
    for k, copy in enumerate(m2_copies):
        copy.wait()
        top = jnp.maximum(top, m2_all[k + 1])
    upper = BOUND_MARGIN * jnp.broadcast_to(jnp.max(top, axis=1, keepdims=True), top.shape)
    lower = LOW_RATIO * upper
    theta = 0.5 * (upper + lower)
    delta = 0.5 * (upper - lower)
    sigma = theta / delta
    damping = 1.0 / sigma
    inv_theta = 1.0 / theta
    coef[0:8] = inv_theta
    rows = []
    for turn in range(1, CHEB):
        following = 1.0 / (2.0 * sigma - damping)
        rows.append((following * damping, 2.0 * following / delta))
        damping = following
    for turn, (a, c2) in enumerate(rows):
        coef[8 + 2 * turn : 9 + 2 * turn] = a[0:1]
        coef[9 + 2 * turn : 10 + 2 * turn] = c2[0:1]
    coef[14:15] = (rows[0][0] * inv_theta + rows[0][1])[0:1]
    coef[15:16] = (rows[0][1] * inv_theta)[0:1]

    alpha, beta, it = bcoef(14), bcoef(15), bcoef(0)

    def combine_plane(i, _):
        for c in range(3):
            d0 = u[0, c, i + 1]
            sol[c, i] = d0 * it
            res[c, i] = rhs[c, i] - r[c, i] * it
            u[0, c, i + 1] = alpha * d0 - beta * u[1, c, i + 1]
        return 0

    lax.fori_loop(0, dx, combine_plane, 0, unroll=UNROLL)
    for c in range(3):
        for p in (0, dx + 1):
            u[0, c, p] = alpha * u[0, c, p] - beta * u[1, c, p]
        for d in (2, 3):
            recv[1, d, c] = alpha[:dx] * recv[0, d, c] - beta[:dx] * recv[1, d, c]

    def step(slot, low, high, a, c2, following):
        other = 1 - slot

        def plane(i, sums):
            v, out = apply_plane(i, slot, low, high)
            inv = invd[i]
            new = []
            for c in range(3):
                rest = res[c, i] - out[c]
                res[c, i] = rest
                sol[c, i] = sol[c, i] + v[c]
                if following is None:
                    new.append(sums[c] + rest)
                    continue
                ahead = c2 * (rest * inv)
                if a is not None:
                    ahead = ahead + a * v[c]
                u[other, c, i + 1] = ahead
                y_send[following, 0, c, pl.ds(i, 1), :] = ahead[dy - 1 : dy]
                y_send[following, 1, c, pl.ds(i, 1), :] = ahead[0:1]
            return tuple(new)

        init = ()
        if following is None:
            init = tuple(jnp.zeros((dy, dz), jnp.float32) for _ in range(3))
        return sweep(plane, following, other, init, SWEEP)

    slot = 0
    for turn in range(1, CHEB):
        low, high = recv_rows(turn)
        if turn + 1 < CHEB:
            step(slot, low, high, bcoef(8 + 2 * turn), bcoef(9 + 2 * turn), turn + 1)
            slot = 1 - slot
            halo_wait(turn + 1, slot)
        else:
            sums = step(slot, low, high, None, None, None)

    c_own[...] = jnp.zeros(c_own.shape, jnp.float32)
    for c in range(3):
        c_own[c : c + 1, :] = jnp.sum(sums[c], axis=0, keepdims=True)
    c_all[g] = c_own[...]
    c_copies = [
        remote(c_own, c_all.at[g], c_ssem.at[k], c_rsem.at[k], group_peer(k))
        for k in range(1, ng)
    ]
    for copy in c_copies:
        copy.start()
    for k in range(1, ng):
        source = lax.rem(g + ng - k, ng)
        remote(c_own, c_all.at[source], c_ssem.at[k], c_rsem.at[k], group_peer(k)).wait()
    cells_z = dz // BLOCK_Z
    size = 3 * cells_z * ng
    flat = c_all[...].reshape(ng * 8, dz)
    li = lax.broadcasted_iota(jnp.int32, (dz, size), 0)
    ki = lax.broadcasted_iota(jnp.int32, (dz, size), 1)
    gather = jnp.where(li // BLOCK_Z == ki % cells_z, 1.0 / (dx * dy * BLOCK_Z), 0.0)
    spread = jnp.dot(flat, gather, precision=HIGHEST, preferred_element_type=jnp.float32)
    ri = lax.broadcasted_iota(jnp.int32, (ng * 8, size), 0)
    kk = lax.broadcasted_iota(jnp.int32, (ng * 8, size), 1) // cells_z
    mine = (ri // 8 == kk // 3) & (ri % 8 == kk % 3)
    vector = jnp.sum(jnp.where(mine, spread, 0.0), axis=0, keepdims=True)
    correction = jnp.sum(inverse[0] * vector, axis=1, keepdims=True)
    bi = lax.broadcasted_iota(jnp.int32, (size, dz), 0)
    bl = lax.broadcasted_iota(jnp.int32, (size, dz), 1)
    table = jnp.where(bi % cells_z == bl // BLOCK_Z, jnp.broadcast_to(correction, (size, dz)), 0.0)
    f_all[...] = jnp.zeros(f_all.shape, jnp.float32)
    for k in range(ng):
        for c in range(3):
            start = (k * 3 + c) * cells_z
            f_all[k + 1, c : c + 1, :] = jnp.sum(
                table[start : start + cells_z], axis=0, keepdims=True
            )
    fx_own[...] = f_all[g + 1]

    def f_copy(d):
        return remote(fx_own, fx_recv.at[d], f_ssem.at[d], f_rsem.at[d], peers[d])

    for d in range(2):
        @pl.when(sends[d])
        def _():
            f_copy(d).start()

    slot = 0

    def fill_plane(i, _):
        for c in range(3):
            u[0, c, i + 1] = jnp.broadcast_to(fx_own[c : c + 1, :], (dy, dz))
        return 0

    lax.fori_loop(0, dx, fill_plane, 0, unroll=UNROLL)
    for d in range(2):
        @pl.when(has[d])
        def _():
            f_copy(d).wait_recv()
        @pl.when(sends[d])
        def _():
            f_copy(d).wait_send()
    for c in range(3):
        u[0, c, 0] = jnp.broadcast_to(fx_recv[0, c : c + 1, :], (dy, dz))
        u[0, c, dx + 1] = jnp.broadcast_to(fx_recv[1, c : c + 1, :], (dy, dz))
    step(
        0,
        lambda c, i: f_all[g, c : c + 1, :],
        lambda c, i: f_all[g + 2, c : c + 1, :],
        None,
        bcoef(0),
        CHEB,
    )
    slot = 1
    for turn in range(CHEB):
        halo_wait(CHEB + turn, slot)
        low, high = recv_rows(CHEB + turn)
        if turn + 1 < CHEB:
            step(slot, low, high, bcoef(8 + 2 * turn), bcoef(9 + 2 * turn), CHEB + turn + 1)
            slot = 1 - slot
        else:
            step(slot, low, high, None, None, None)


def per_device(rhs, material, level, mortar, mu, lam, inverse):
    nb = lax.axis_size("bricks")
    ng = lax.axis_size("group")
    dx, dy, dz = material.shape
    f32 = jnp.float32
    vmem = pl.BlockSpec(memory_space=pltpu.VMEM)
    smem = pl.BlockSpec(memory_space=pltpu.SMEM)
    dma = pltpu.SemaphoreType.DMA
    grid = pltpu.VMEM((dx, dy, dz), f32)
    scratch = [
        pltpu.VMEM((2, 3, dx + 2, dy, dz), f32),
        pltpu.VMEM((3, dx, dy, dz), f32),
        pltpu.VMEM((dx + 2, dy, dz), f32),
        pltpu.VMEM((dx + 1, dy, dz), f32),
        grid, grid, grid, grid, grid, grid, grid,
        pltpu.VMEM((16, dz), f32),
        pltpu.SMEM((dy,), jnp.int32),
        pltpu.VMEM((dy, dz), f32),
        pltpu.VMEM((2, dx, dz), f32),
        pltpu.VMEM((4, dx, dz), f32),
        pltpu.VMEM((3, dy, dz), f32),
        pltpu.VMEM((ROUNDS, 3, dy, dz), f32),
        pltpu.VMEM((ROUNDS, 2, 3, dx, dz), f32),
        pltpu.VMEM((ROUNDS, 4, 3, dx, dz), f32),
        pltpu.VMEM((8, dz), f32),
        pltpu.VMEM((ng, 8, dz), f32),
        pltpu.VMEM((8, dz), f32),
        pltpu.VMEM((nb, 8, dz), f32),
        pltpu.VMEM((8, dz), f32),
        pltpu.VMEM((ng, 8, dz), f32),
        pltpu.VMEM((ng + 2, 8, dz), f32),
        pltpu.VMEM((8, dz), f32),
        pltpu.VMEM((2, 8, dz), f32),
        dma((4,)), dma((4,)),
        dma((ROUNDS, 4)), dma((ROUNDS, 4)),
        dma((ng,)), dma((ng,)),
        dma((nb,)), dma((nb,)),
        dma((ng,)), dma((ng,)),
        dma((2,)), dma((2,)),
    ]
    return pl.pallas_call(
        functools.partial(kernel, nb, ng, dx, dy, dz),
        out_shape=(
            jax.ShapeDtypeStruct(rhs.shape, f32),
            jax.ShapeDtypeStruct(rhs.shape, f32),
        ),
        in_specs=[vmem, vmem, vmem, smem, smem, smem, vmem],
        out_specs=(vmem, vmem),
        scratch_shapes=scratch,
        compiler_params=pltpu.CompilerParams(
            collective_id=0, has_side_effects=True, vmem_limit_bytes=16 * 2**20
        ),
    )(rhs, material, level, mortar, mu, lam, inverse)


def solution(mesh):
    return jax.shard_map(
        per_device,
        mesh=mesh,
        in_specs=(
            P(None, "bricks", "group", None),
            P("bricks", "group", None),
            P("bricks", "group"),
            P("bricks", "group", None),
            P(),
            P(),
            P("bricks", None, None),
        ),
        out_specs=(P(None, "bricks", "group", None), P(None, "bricks", "group", None)),
        check_vma=False,
    )
```

```python
import functools

import jax
import jax.numpy as jnp
from jax import lax
from jax.experimental import pallas as pl
from jax.experimental.pallas import tpu as pltpu
from jax.sharding import PartitionSpec as P

BLOCK_Z = 32
CHEB = 4
LOW_RATIO = 0.15
BOUND_MARGIN = 1.1
ROUNDS = 2 * CHEB
UNROLL = 4
SWEEP = 7
HIGHEST = lax.Precision.HIGHEST


def kernel(
    nb, ng, dx, dy, dz,
    rhs_in, material_in, level, mortar, mu, lam, inverse_in,
    sol, res, rhs, material, inverse,
    u, r, shear, wx, wyp, wym, wzp, wzm, dg, hb, invd, coef, undo,
    s_send_up, s_send_y, s_recv, above, up_send, y_send, recv,
    m_own, m_all, m2_own, m2_all, c_own, c_all, f_all, inv_recv, pack_send, pack_top, pack_recv, in_sem,
    s_ssem, s_rsem, h_ssem, h_rsem,
    m_ssem, m_rsem, m2_ssem, m2_rsem, c_ssem, c_rsem, p_ssem, p_rsem, i_ssem, i_rsem,
):
    b = lax.axis_index("bricks")
    g = lax.axis_index("group")
    has = [b > 0, b < nb - 1, g > 0, g < ng - 1]
    sends = [has[1], has[0], has[3], has[2]]
    peers = [(b + 1, g), (b - 1, g), (b, g + 1), (b, g - 1)]

    def remote(src, dst, ssem, rsem, peer):
        return pltpu.make_async_remote_copy(
            src_ref=src, dst_ref=dst, send_sem=ssem, recv_sem=rsem,
            device_id=peer, device_id_type=pl.DeviceIdType.MESH,
        )

    barrier = pltpu.get_barrier_semaphore()
    others = [(b, lax.rem(g + k, ng)) for k in range(1, ng)]
    others += [(lax.rem(b + k, nb), g) for k in range(1, nb)]
    around = [(lax.rem(g + k, ng)) for k in range(1, ng)]
    for peer in others:
        pl.semaphore_signal(
            barrier, inc=1, device_id=peer, device_id_type=pl.DeviceIdType.MESH
        )
    for d in range(2):
        @pl.when(has[d])
        def _():
            for at in around:
                pl.semaphore_signal(
                    barrier, inc=1, device_id=(b - 1 + 2 * d, at),
                    device_id_type=pl.DeviceIdType.MESH,
                )

    def fetch(k):
        source = [material_in, rhs_in, inverse_in.at[0]][k]
        return pltpu.make_async_copy(source, [material, rhs, inverse][k], in_sem.at[k])

    for k in range(3):
        fetch(k).start()

    grade = jnp.broadcast_to(level[...], (dy, dz))
    scale = jnp.where(grade == 0, 1.0, jnp.where(grade == 1, 4.0, 16.0))
    zero_face = jnp.zeros((3, dx, dz), jnp.float32)

    order = [mortar[0, 0, k] for k in range(dy)]
    for k in range(dy):
        total = jnp.int32(0)
        for j in range(dy):
            total = jnp.where(order[j] == k, jnp.int32(j), total)
        undo[k] = total

    def lookup(ids, table):
        total = jnp.where(ids == 0, table[0], 0.0)
        for entry in range(1, 4):
            total = jnp.where(ids == entry, table[entry], total)
        return total * scale

    def shear_plane(i, _):
        ids = material[i]
        plane = lookup(ids, mu)
        shear[i + 1] = plane
        hb[i] = lookup(ids, lam)
        s_send_y[0, pl.ds(i, 1), :] = plane[dy - 1 : dy]
        s_send_y[1, pl.ds(i, 1), :] = plane[0:1]
        return 0

    for k in range(3):
        fetch(k).wait()
    lax.fori_loop(0, dx, shear_plane, 0, unroll=UNROLL)
    for k in range(dy):
        s_send_up[k : k + 1, :] = shear[dx, pl.ds(order[k], 1), :]

    both = jnp.where(has[0], len(around), 0) + jnp.where(has[1], len(around), 0)
    pl.semaphore_wait(barrier, len(others) + both)

    def s_copy(d):
        src = [s_send_up, shear.at[1], s_send_y.at[0], s_send_y.at[1]][d]
        return remote(src, s_recv.at[d], s_ssem.at[d], s_rsem.at[d], peers[d])

    def exchange_start(copy, directions=(0, 1, 2, 3)):
        for d in directions:
            @pl.when(sends[d])
            def _():
                copy(d).start()

    def exchange_wait(copy, directions=(0, 1, 2, 3)):
        for d in directions:
            @pl.when(has[d])
            def _():
                copy(d).wait_recv()
        for d in directions:
            @pl.when(sends[d])
            def _():
                copy(d).wait_send()

    exchange_start(s_copy)

    @pl.when(b == 0)
    def _():
        s_recv[0] = shear[1]

    @pl.when(b == nb - 1)
    def _():
        shear[dx + 1] = shear[dx]
        s_recv[1] = shear[dx]

    @pl.when(g == 0)
    def _():
        s_recv[2] = s_send_y[1]

    @pl.when(g == ng - 1)
    def _():
        s_recv[3] = s_send_y[0]

    for d in range(4):
        @pl.when(jnp.logical_not(has[d]))
        def _():
            for turn in range(ROUNDS):
                recv[turn, d] = zero_face
            pack_recv[d] = jnp.zeros(pack_recv.shape[1:], jnp.float32)
            if d < 2:
                inv_recv[d] = jnp.zeros(inv_recv.shape[1:], jnp.float32)
                c_all[2 * d] = jnp.zeros(c_all.shape[1:], jnp.float32)

    exchange_wait(s_copy)
    shear[0] = s_recv[0]

    @pl.when(b < nb - 1)
    def _():
        for k in range(dy):
            shear[dx + 1, k : k + 1, :] = s_recv[1, pl.ds(undo[k], 1), :]

    row = lax.broadcasted_iota(jnp.int32, (dy, dz), 0)
    lane = lax.broadcasted_iota(jnp.int32, (dy, dz), 1)

    def y_near(v, low, high):
        ym = jnp.where(row == 0, jnp.broadcast_to(low, v.shape), pltpu.roll(v, 1, 0))
        yp = jnp.where(
            row == dy - 1, jnp.broadcast_to(high, v.shape), pltpu.roll(v, dy - 1, 0)
        )
        return ym, yp

    def z_near(v):
        return pltpu.roll(v, 1, 1), pltpu.roll(v, dz - 1, 1)

    def h_copy(turn, slot):
        def copy(d):
            src = [
                up_send.at[turn], u.at[slot, :, 1], y_send.at[turn, 0], y_send.at[turn, 1]
            ][d]
            return remote(
                src, recv.at[turn, d], h_ssem.at[turn, d], h_rsem.at[turn, d], peers[d]
            )
        return copy

    def sweep(plane, turn, slot, carry, unroll):
        carry = plane(0, carry)
        carry = plane(dx - 1, carry)
        if turn is not None:
            for c in range(3):
                for k in range(dy):
                    up_send[turn, c, k : k + 1, :] = u[slot, c, dx, pl.ds(order[k], 1), :]
            exchange_start(h_copy(turn, slot), (0, 1))
        carry = lax.fori_loop(1, dx - 1, plane, carry, unroll=unroll)
        if turn is not None:
            exchange_start(h_copy(turn, slot), (2, 3))
        return carry

    wx[0] = 0.5 * (shear[0] + shear[1])
    wx[dx] = 0.5 * (shear[dx] + shear[dx + 1])

    def weight_plane(i, best):
        s = shear[i + 1]
        xp = 0.5 * (s + shear[i + 2])
        wx[i + 1] = xp
        xm = 0.5 * (s + shear[i])
        ym, yp = y_near(s, s_recv[2, pl.ds(i, 1), :], s_recv[3, pl.ds(i, 1), :])
        ym = 0.5 * (s + ym)
        yp = 0.5 * (s + yp)
        zm, zp = z_near(s)
        zm = 0.5 * (s + zm)
        zp = 0.5 * (s + zp)
        wyp[i] = yp
        wym[i] = ym
        wzp[i] = jnp.where(lane == dz - 1, 0.0, zp)
        wzm[i] = jnp.where(lane == 0, 0.0, zm)
        total = xp + xm + yp + ym + jnp.where(lane == dz - 1, s, zp) + jnp.where(lane == 0, s, zm)
        bulk = hb[i]
        diagonal = total + 1.5 * bulk
        inv = 1.0 / diagonal
        invd[i] = inv
        dg[i] = total + bulk
        half = 0.5 * bulk
        hb[i] = half
        none = jnp.zeros((1, dz), jnp.float32)
        for d, y in ((2, dy - 1), (3, 0)):
            pack_send[d, 0, pl.ds(i, 1), :] = inv[y : y + 1]
            pack_send[d, 1, pl.ds(i, 1), :] = half[y : y + 1]
            first, last = isinstance(i, int) and i == 0, isinstance(i, int) and i == dx - 1
            pack_send[d, 2, pl.ds(i, 1), :] = xm[y : y + 1] if first else none
            pack_send[d, 3, pl.ds(i, 1), :] = xp[y : y + 1] if last else none
        if isinstance(i, int):
            planes = (inv, half, jnp.where(row == 0, ym, 0.0), jnp.where(row == dy - 1, yp, 0.0))
            for k, value in enumerate(planes):
                if i == 0:
                    pack_send[1, k] = value
                else:
                    pack_top[k] = value
        for c in range(3):
            d0 = rhs[c, i] * inv
            u[0, c, i + 1] = d0
            y_send[0, 0, c, pl.ds(i, 1), :] = d0[dy - 1 : dy]
            y_send[0, 1, c, pl.ds(i, 1), :] = d0[0:1]
        return jnp.maximum(best, (2.0 * total + 2.5 * bulk) / diagonal)

    best = sweep(weight_plane, 0, 0, jnp.zeros((dy, dz), jnp.float32), 2)
    m_own[...] = jnp.broadcast_to(jnp.max(best, axis=0, keepdims=True), m_own.shape)

    def halo_wait(turn, slot):
        exchange_wait(h_copy(turn, slot))
        place_halo(turn, slot)

    def place_halo(turn, slot):
        for c in range(3):
            u[slot, c, 0] = recv[turn, 0, c]
            above[c] = recv[turn, 1, c]
        for c in range(3):
            for k in range(dy):
                u[slot, c, dx + 1, k : k + 1, :] = above[c, pl.ds(undo[k], 1), :]

    def apply_plane(i, slot, low, high):
        v = [u[slot, c, i + 1] for c in range(3)]
        coupled = hb[i] * (v[0] + v[1] + v[2])
        out = []
        for c in range(3):
            ym, yp = y_near(v[c], low(c, i), high(c, i))
            zm, zp = z_near(v[c])
            near = wx[i] * u[slot, c, i] + wx[i + 1] * u[slot, c, i + 2]
            near = near + wym[i] * ym + wyp[i] * yp + wzm[i] * zm + wzp[i] * zp
            out.append(dg[i] * v[c] + coupled - near)
        return v, out

    def recv_rows(turn):
        return (
            lambda c, i: recv[turn, 2, c, pl.ds(i, 1), :],
            lambda c, i: recv[turn, 3, c, pl.ds(i, 1), :],
        )

    def bcoef(k):
        return jnp.broadcast_to(coef[k : k + 1, :], (dy, dz))

    def ring_start(own, store, ssem, rsem, peer_of, count, mine):
        copies = []
        for k in range(1, count):
            copies.append(remote(own, store.at[k], ssem.at[k], rsem.at[k], peer_of(k)))
        for copy in copies:
            copy.start()
        return copies

    group_peer = lambda k: (b, lax.rem(g + k, ng))
    brick_peer = lambda k: (lax.rem(b + k, nb), g)

    m_copies = ring_start(m_own, m_all, m_ssem, m_rsem, group_peer, ng, g)
    halo_wait(0, 0)

    low, high = recv_rows(0)

    def first_plane(i, _):
        _, out = apply_plane(i, 0, low, high)
        inv = invd[i]
        for c in range(3):
            r[c, i] = out[c]
            q = out[c] * inv
            u[1, c, i + 1] = q
            y_send[1, 0, c, pl.ds(i, 1), :] = q[dy - 1 : dy]
            y_send[1, 1, c, pl.ds(i, 1), :] = q[0:1]
        return 0

    sweep(first_plane, 1, 1, 0, SWEEP)

    def p_copy(d):
        return remote(
            pack_send.at[d], pack_recv.at[d], p_ssem.at[d], p_rsem.at[d], peers[d]
        )

    for q in range(4):
        for k in range(dy):
            pack_send[0, q, k : k + 1, :] = pack_top[q, pl.ds(order[k], 1), :]
    top = m_own[...]
    for k, copy in enumerate(m_copies):
        copy.wait()
        top = jnp.maximum(top, m_all[k + 1])
    m2_own[...] = top
    m2_copies = ring_start(m2_own, m2_all, m2_ssem, m2_rsem, brick_peer, nb, b)
    exchange_start(p_copy)
    halo_wait(1, 1)
    for k, copy in enumerate(m2_copies):
        copy.wait()
        top = jnp.maximum(top, m2_all[k + 1])
    upper = BOUND_MARGIN * jnp.broadcast_to(jnp.max(top, axis=1, keepdims=True), top.shape)
    lower = LOW_RATIO * upper
    theta = 0.5 * (upper + lower)
    delta = 0.5 * (upper - lower)
    sigma = theta / delta
    damping = 1.0 / sigma
    inv_theta = 1.0 / theta
    coef[0:8] = inv_theta
    rows = []
    for turn in range(1, CHEB):
        following = 1.0 / (2.0 * sigma - damping)
        rows.append((following * damping, 2.0 * following / delta))
        damping = following
    for turn, (a, c2) in enumerate(rows):
        coef[8 + 2 * turn : 9 + 2 * turn] = a[0:1]
        coef[9 + 2 * turn : 10 + 2 * turn] = c2[0:1]
    coef[14:15] = (rows[0][0] * inv_theta + rows[0][1])[0:1]
    coef[15:16] = (rows[0][1] * inv_theta)[0:1]

    alpha, beta, it = bcoef(14), bcoef(15), bcoef(0)

    def combine_plane(i, _):
        for c in range(3):
            d0 = u[0, c, i + 1]
            sol[c, i] = d0 * it
            res[c, i] = rhs[c, i] - r[c, i] * it
            u[0, c, i + 1] = alpha * d0 - beta * u[1, c, i + 1]
        return 0

    lax.fori_loop(0, dx, combine_plane, 0, unroll=UNROLL)
    for c in range(3):
        for p in (0, dx + 1):
            u[0, c, p] = alpha * u[0, c, p] - beta * u[1, c, p]
        for d in (2, 3):
            recv[1, d, c] = alpha[:dx] * recv[0, d, c] - beta[:dx] * recv[1, d, c]

    def step(slot, low, high, a, c2, following, summed=False, send=True):
        other = 1 - slot

        def plane(i, sums):
            v, out = apply_plane(i, slot, low, high)
            inv = invd[i]
            new = []
            for c in range(3):
                rest = res[c, i] - out[c]
                res[c, i] = rest
                sol[c, i] = sol[c, i] + v[c]
                if summed:
                    new.append(sums[c] + rest)
                if following is None:
                    continue
                ahead = c2 * (rest * inv)
                if a is not None:
                    ahead = ahead + a * v[c]
                u[other, c, i + 1] = ahead
                if not send:
                    continue
                y_send[following, 0, c, pl.ds(i, 1), :] = ahead[dy - 1 : dy]
                y_send[following, 1, c, pl.ds(i, 1), :] = ahead[0:1]
            return tuple(new)

        init = ()
        if summed:
            init = tuple(jnp.zeros((dy, dz), jnp.float32) for _ in range(3))
        return sweep(plane, following if send else None, other, init, SWEEP)

    def i_copy(d):
        return remote(inverse, inv_recv.at[d], i_ssem.at[d], i_rsem.at[d], peers[d])

    slot = 0
    for turn in range(1, CHEB):
        low, high = recv_rows(turn)
        if turn + 1 < CHEB:
            step(slot, low, high, bcoef(8 + 2 * turn), bcoef(9 + 2 * turn), turn + 1)
            slot = 1 - slot
            if turn == 1:
                exchange_start(i_copy, (0, 1))
            halo_wait(turn + 1, slot)
        else:
            sums = step(slot, low, high, None, bcoef(0), CHEB, summed=True)

    c_own[...] = jnp.zeros(c_own.shape, jnp.float32)
    for c in range(3):
        c_own[c : c + 1, :] = jnp.sum(sums[c], axis=0, keepdims=True)
    c_all[1, g] = c_own[...]

    def c_copy(q, k):
        slot = q * ng + k
        return remote(
            c_own, c_all.at[q, g], c_ssem.at[slot], c_rsem.at[slot],
            (b + 1 - q, lax.rem(g + k, ng)),
        )

    def c_arrival(q, k):
        slot = q * ng + k
        source = lax.rem(g + ng - k, ng)
        return remote(
            c_own, c_all.at[q, source], c_ssem.at[slot], c_rsem.at[slot],
            (b + 1 - q, lax.rem(g + k, ng)),
        )

    def coarse_all(to_do, flags):
        for q in (0, 2, 1):
            first = 1 if q == 1 else 0
            if q == 1:
                for k in range(first, ng):
                    to_do(q, k)
                continue

            @pl.when(flags[q])
            def _():
                for k in range(first, ng):
                    to_do(q, k)

    coarse_all(lambda q, k: c_copy(q, k).start(), {0: has[1], 2: has[0]})
    f_all[...] = jnp.zeros(f_all.shape, jnp.float32)
    exchange_wait(p_copy)
    exchange_wait(i_copy, (0, 1))
    coarse_all(lambda q, k: c_arrival(q, k).wait_recv(), {0: has[0], 2: has[1]})
    coarse_all(lambda q, k: c_copy(q, k).wait_send(), {0: has[1], 2: has[0]})

    cells_z = dz // BLOCK_Z
    size = 3 * cells_z * ng
    flat = c_all[...].reshape(3 * ng * 8, dz)
    li = lax.broadcasted_iota(jnp.int32, (dz, size), 0)
    ki = lax.broadcasted_iota(jnp.int32, (dz, size), 1)
    gather = jnp.where(li // BLOCK_Z == ki % cells_z, 1.0 / (dx * dy * BLOCK_Z), 0.0)
    spread = jnp.dot(flat, gather, precision=HIGHEST, preferred_element_type=jnp.float32)
    ri = lax.broadcasted_iota(jnp.int32, (ng * 8, size), 0)
    kk = lax.broadcasted_iota(jnp.int32, (ng * 8, size), 1) // cells_z
    mine = (ri // 8 == kk // 3) & (ri % 8 == kk % 3)
    bi = lax.broadcasted_iota(jnp.int32, (size, dz), 0)
    bl = lax.broadcasted_iota(jnp.int32, (size, dz), 1)
    placed = bi % cells_z == bl // BLOCK_Z
    for q in range(3):
        part = spread[q * ng * 8 : (q + 1) * ng * 8]
        vector = jnp.sum(jnp.where(mine, part, 0.0), axis=0, keepdims=True)
        matrix = inverse[...] if q == 1 else inv_recv[q // 2]
        correction = jnp.sum(matrix * vector, axis=1, keepdims=True)
        table = jnp.where(placed, jnp.broadcast_to(correction, (size, dz)), 0.0)
        for k in range(ng):
            for c in range(3):
                start = (k * 3 + c) * cells_z
                f_all[q, k + 1, c : c + 1, :] = jnp.sum(
                    table[start : start + cells_z], axis=0, keepdims=True
                )

    def full(q, at, c):
        return jnp.broadcast_to(f_all[q, at, c : c + 1, :], (dy, dz))

    own_fine = [full(1, g + 1, c) for c in range(3)]

    def fill_plane(i, _):
        for c in range(3):
            u[0, c, i + 1] = own_fine[c]
        return 0

    lax.fori_loop(0, dx, fill_plane, 0, unroll=UNROLL)
    for c in range(3):
        u[0, c, 0] = full(0, g + 1, c)
        u[0, c, dx + 1] = full(2, g + 1, c)
    it = bcoef(0)
    exchange_wait(h_copy(CHEB, 1))
    step(
        0,
        lambda c, i: f_all[1, g, c : c + 1, :],
        lambda c, i: f_all[1, g + 2, c : c + 1, :],
        None,
        it,
        CHEB,
        send=False,
    )

    def fine_on_face(d, near, cross, here, before, after):
        inv, half, w_low, w_high = [pack_recv[d, k] for k in range(4)]
        zm, zp = z_near(near)
        zm = jnp.where(lane == 0, 0.0, 0.5 * (near + zm))
        zp = jnp.where(lane == dz - 1, 0.0, 0.5 * (near + zp))
        rim = jnp.where((lane == 0) | (lane == dz - 1), near, 0.0)
        weight = 2.0 * half + cross + w_low + w_high + zm + zp + rim
        values = [full(*here, c) for c in range(3)]
        coupled = half * (values[0] + values[1] + values[2])
        for c in range(3):
            fm, fp = z_near(values[c])
            applied = weight * values[c] + coupled - cross * own_fine[c]
            applied = applied - zm * fm - zp * fp
            applied = applied - w_low * full(*before, c) - w_high * full(*after, c)
            recv[CHEB, d, c] = recv[CHEB, d, c] - it * (inv * applied)

    fine_on_face(0, s_recv[0], wx[0], (0, g + 1), (0, g), (0, g + 2))
    fine_on_face(1, s_recv[1], 0.5 * (s_recv[1] + s_send_up[...]), (2, g + 1), (2, g), (2, g + 2))
    fine_on_face(2, s_recv[2], 0.5 * (s_recv[2] + s_send_y[1]), (1, g), (0, g), (2, g))
    fine_on_face(3, s_recv[3], 0.5 * (s_recv[3] + s_send_y[0]), (1, g + 2), (0, g + 2), (2, g + 2))
    place_halo(CHEB, 1)

    slot = 1
    for turn in range(CHEB):
        if turn > 0:
            halo_wait(CHEB + turn, slot)
        low, high = recv_rows(CHEB + turn)
        if turn + 1 < CHEB:
            step(slot, low, high, bcoef(8 + 2 * turn), bcoef(9 + 2 * turn), CHEB + turn + 1)
            slot = 1 - slot
        else:
            step(slot, low, high, None, None, None)


def per_device(rhs, material, level, mortar, mu, lam, inverse):
    nb = lax.axis_size("bricks")
    ng = lax.axis_size("group")
    dx, dy, dz = material.shape
    f32 = jnp.float32
    vmem = pl.BlockSpec(memory_space=pltpu.VMEM)
    smem = pl.BlockSpec(memory_space=pltpu.SMEM)
    hbm = pl.BlockSpec(memory_space=pltpu.HBM)
    dma = pltpu.SemaphoreType.DMA
    grid = pltpu.VMEM((dx, dy, dz), f32)
    cg = inverse.shape[1]
    scratch = [
        pltpu.VMEM((3, dx, dy, dz), f32),
        pltpu.VMEM((dx, dy, dz), jnp.int32),
        pltpu.VMEM((cg, cg), f32),
        pltpu.VMEM((2, 3, dx + 2, dy, dz), f32),
        pltpu.VMEM((3, dx, dy, dz), f32),
        pltpu.VMEM((dx + 2, dy, dz), f32),
        pltpu.VMEM((dx + 1, dy, dz), f32),
        grid, grid, grid, grid, grid, grid, grid,
        pltpu.VMEM((16, dz), f32),
        pltpu.SMEM((dy,), jnp.int32),
        pltpu.VMEM((dy, dz), f32),
        pltpu.VMEM((2, dx, dz), f32),
        pltpu.VMEM((4, dx, dz), f32),
        pltpu.VMEM((3, dy, dz), f32),
        pltpu.VMEM((ROUNDS, 3, dy, dz), f32),
        pltpu.VMEM((ROUNDS, 2, 3, dx, dz), f32),
        pltpu.VMEM((ROUNDS, 4, 3, dx, dz), f32),
        pltpu.VMEM((8, dz), f32),
        pltpu.VMEM((ng, 8, dz), f32),
        pltpu.VMEM((8, dz), f32),
        pltpu.VMEM((nb, 8, dz), f32),
        pltpu.VMEM((8, dz), f32),
        pltpu.VMEM((3, ng, 8, dz), f32),
        pltpu.VMEM((3, ng + 2, 8, dz), f32),
        pltpu.VMEM((2, cg, cg), f32),
        pltpu.VMEM((4, 4, dx, dz), f32),
        pltpu.VMEM((4, dy, dz), f32),
        pltpu.VMEM((4, 4, dx, dz), f32),
        dma((3,)),
        dma((4,)), dma((4,)),
        dma((ROUNDS, 4)), dma((ROUNDS, 4)),
        dma((ng,)), dma((ng,)),
        dma((nb,)), dma((nb,)),
        dma((3 * ng,)), dma((3 * ng,)),
        dma((4,)), dma((4,)),
        dma((2,)), dma((2,)),
    ]
    return pl.pallas_call(
        functools.partial(kernel, nb, ng, dx, dy, dz),
        out_shape=(
            jax.ShapeDtypeStruct(rhs.shape, f32),
            jax.ShapeDtypeStruct(rhs.shape, f32),
        ),
        in_specs=[hbm, hbm, vmem, smem, smem, smem, hbm],
        out_specs=(vmem, vmem),
        scratch_shapes=scratch,
        compiler_params=pltpu.CompilerParams(
            collective_id=0, has_side_effects=True, vmem_limit_bytes=16 * 2**20
        ),
    )(rhs, material, level, mortar, mu, lam, inverse)


def solution(mesh):
    return jax.shard_map(
        per_device,
        mesh=mesh,
        in_specs=(
            P(None, "bricks", "group", None),
            P("bricks", "group", None),
            P("bricks", "group"),
            P("bricks", "group", None),
            P(),
            P(),
            P("bricks", None, None),
        ),
        out_specs=(P(None, "bricks", "group", None), P(None, "bricks", "group", None)),
        check_vma=False,
    )
```

```python
import functools

import jax
import jax.numpy as jnp
from jax import lax
from jax.experimental import pallas as pl
from jax.experimental.pallas import tpu as pltpu
from jax.sharding import PartitionSpec as P

BLOCK_Z = 32
CHEB = 4
LOW_RATIO = 0.15
BOUND_MARGIN = 1.1
ROUNDS = 2 * CHEB
UNROLL = 4
SWEEP = 7
HIGHEST = lax.Precision.HIGHEST


def kernel(
    nb, ng, dx, dy, dz,
    rhs_in, material_in, level, mortar, mu, lam, inverse_in,
    sol, res, rhs, material, inverse,
    u, r, shear, wx, wyp, wym, wzp, wzm, dg, hb, invd, coef, undo,
    s_send_up, s_send_y, s_recv, above, up_send, y_send, recv,
    m_own, m_all, m2_own, m2_all, c_own, c_all, f_all, inv_recv, pack_send, pack_top, pack_recv, in_sem,
    s_ssem, s_rsem, h_ssem, h_rsem,
    m_ssem, m_rsem, m2_ssem, m2_rsem, c_ssem, c_rsem, p_ssem, p_rsem, i_ssem, i_rsem,
):
    b = lax.axis_index("bricks")
    g = lax.axis_index("group")
    has = [b > 0, b < nb - 1, g > 0, g < ng - 1]
    sends = [has[1], has[0], has[3], has[2]]
    peers = [(b + 1, g), (b - 1, g), (b, g + 1), (b, g - 1)]

    def remote(src, dst, ssem, rsem, peer):
        return pltpu.make_async_remote_copy(
            src_ref=src, dst_ref=dst, send_sem=ssem, recv_sem=rsem,
            device_id=peer, device_id_type=pl.DeviceIdType.MESH,
        )

    barrier = pltpu.get_barrier_semaphore()
    others = [(b, lax.rem(g + k, ng)) for k in range(1, ng)]
    others += [(lax.rem(b + k, nb), g) for k in range(1, nb)]
    around = [(lax.rem(g + k, ng)) for k in range(1, ng)]
    for peer in others:
        pl.semaphore_signal(
            barrier, inc=1, device_id=peer, device_id_type=pl.DeviceIdType.MESH
        )
    for d in range(2):
        @pl.when(has[d])
        def _():
            for at in around:
                pl.semaphore_signal(
                    barrier, inc=1, device_id=(b - 1 + 2 * d, at),
                    device_id_type=pl.DeviceIdType.MESH,
                )

    def fetch(k):
        source = [material_in, rhs_in, inverse_in.at[0]][k]
        return pltpu.make_async_copy(source, [material, rhs, inverse][k], in_sem.at[k])

    for k in range(3):
        fetch(k).start()

    grade = jnp.broadcast_to(level[...], (dy, dz))
    scale = jnp.where(grade == 0, 1.0, jnp.where(grade == 1, 4.0, 16.0))
    zero_face = jnp.zeros((3, dx, dz), jnp.float32)

    order = [mortar[0, 0, k] for k in range(dy)]
    for k in range(dy):
        total = jnp.int32(0)
        for j in range(dy):
            total = jnp.where(order[j] == k, jnp.int32(j), total)
        undo[k] = total

    def lookup(ids, table):
        total = jnp.where(ids == 0, table[0], 0.0)
        for entry in range(1, 4):
            total = jnp.where(ids == entry, table[entry], total)
        return total * scale

    def shear_plane(i, _):
        ids = material[i]
        plane = lookup(ids, mu)
        shear[i + 1] = plane
        hb[i] = lookup(ids, lam)
        s_send_y[0, pl.ds(i, 1), :] = plane[dy - 1 : dy]
        s_send_y[1, pl.ds(i, 1), :] = plane[0:1]
        return 0

    for k in range(3):
        fetch(k).wait()
    lax.fori_loop(0, dx, shear_plane, 0, unroll=UNROLL)
    for k in range(dy):
        s_send_up[k : k + 1, :] = shear[dx, pl.ds(order[k], 1), :]

    both = jnp.where(has[0], len(around), 0) + jnp.where(has[1], len(around), 0)
    pl.semaphore_wait(barrier, len(others) + both)

    def s_copy(d):
        src = [s_send_up, shear.at[1], s_send_y.at[0], s_send_y.at[1]][d]
        return remote(src, s_recv.at[d], s_ssem.at[d], s_rsem.at[d], peers[d])

    def exchange_start(copy, directions=(0, 1, 2, 3)):
        for d in directions:
            @pl.when(sends[d])
            def _():
                copy(d).start()

    def exchange_wait(copy, directions=(0, 1, 2, 3)):
        for d in directions:
            @pl.when(has[d])
            def _():
                copy(d).wait_recv()
        for d in directions:
            @pl.when(sends[d])
            def _():
                copy(d).wait_send()

    exchange_start(s_copy)

    @pl.when(b == 0)
    def _():
        s_recv[0] = shear[1]

    @pl.when(b == nb - 1)
    def _():
        shear[dx + 1] = shear[dx]
        s_recv[1] = shear[dx]

    @pl.when(g == 0)
    def _():
        s_recv[2] = s_send_y[1]

    @pl.when(g == ng - 1)
    def _():
        s_recv[3] = s_send_y[0]

    for d in range(4):
        @pl.when(jnp.logical_not(has[d]))
        def _():
            for turn in range(ROUNDS):
                recv[turn, d] = zero_face
            pack_recv[d] = jnp.zeros(pack_recv.shape[1:], jnp.float32)
            if d < 2:
                inv_recv[d] = jnp.zeros(inv_recv.shape[1:], jnp.float32)
                c_all[2 * d] = jnp.zeros(c_all.shape[1:], jnp.float32)

    exchange_wait(s_copy)
    shear[0] = s_recv[0]

    @pl.when(b < nb - 1)
    def _():
        for k in range(dy):
            shear[dx + 1, k : k + 1, :] = s_recv[1, pl.ds(undo[k], 1), :]

    row = lax.broadcasted_iota(jnp.int32, (dy, dz), 0)
    lane = lax.broadcasted_iota(jnp.int32, (dy, dz), 1)

    def y_near(v, low, high):
        ym = jnp.where(row == 0, jnp.broadcast_to(low, v.shape), pltpu.roll(v, 1, 0))
        yp = jnp.where(
            row == dy - 1, jnp.broadcast_to(high, v.shape), pltpu.roll(v, dy - 1, 0)
        )
        return ym, yp

    def z_near(v):
        return pltpu.roll(v, 1, 1), pltpu.roll(v, dz - 1, 1)

    def h_copy(turn, slot):
        def copy(d):
            src = [
                up_send.at[turn], u.at[slot, :, 1], y_send.at[turn, 0], y_send.at[turn, 1]
            ][d]
            return remote(
                src, recv.at[turn, d], h_ssem.at[turn, d], h_rsem.at[turn, d], peers[d]
            )
        return copy

    even = lax.rem(b, 2) == 0

    def sweep(plane, turn, slot, carry, unroll):
        carry = plane(0, carry)
        carry = plane(dx - 1, carry)
        if turn is not None:
            copy = h_copy(turn, slot)

            @pl.when(sends[1] & even)
            def _():
                copy(1).start()

            for c in range(3):
                for k in range(dy):
                    up_send[turn, c, k : k + 1, :] = u[slot, c, dx, pl.ds(order[k], 1), :]
            exchange_start(copy, (0,))

            @pl.when(sends[1] & jnp.logical_not(even))
            def _():
                copy(1).start()

        carry = lax.fori_loop(1, dx - 1, plane, carry, unroll=unroll)
        if turn is not None:
            exchange_start(h_copy(turn, slot), (2, 3))
        return carry

    wx[0] = 0.5 * (shear[0] + shear[1])
    wx[dx] = 0.5 * (shear[dx] + shear[dx + 1])

    def weight_plane(i, best):
        s = shear[i + 1]
        xp = 0.5 * (s + shear[i + 2])
        wx[i + 1] = xp
        xm = 0.5 * (s + shear[i])
        ym, yp = y_near(s, s_recv[2, pl.ds(i, 1), :], s_recv[3, pl.ds(i, 1), :])
        ym = 0.5 * (s + ym)
        yp = 0.5 * (s + yp)
        zm, zp = z_near(s)
        zm = 0.5 * (s + zm)
        zp = 0.5 * (s + zp)
        wyp[i] = yp
        wym[i] = ym
        wzp[i] = jnp.where(lane == dz - 1, 0.0, zp)
        wzm[i] = jnp.where(lane == 0, 0.0, zm)
        total = xp + xm + yp + ym + jnp.where(lane == dz - 1, s, zp) + jnp.where(lane == 0, s, zm)
        bulk = hb[i]
        diagonal = total + 1.5 * bulk
        inv = 1.0 / diagonal
        invd[i] = inv
        dg[i] = total + bulk
        half = 0.5 * bulk
        hb[i] = half
        none = jnp.zeros((1, dz), jnp.float32)
        for d, y in ((2, dy - 1), (3, 0)):
            pack_send[d, 0, pl.ds(i, 1), :] = inv[y : y + 1]
            pack_send[d, 1, pl.ds(i, 1), :] = half[y : y + 1]
            first, last = isinstance(i, int) and i == 0, isinstance(i, int) and i == dx - 1
            pack_send[d, 2, pl.ds(i, 1), :] = xm[y : y + 1] if first else none
            pack_send[d, 3, pl.ds(i, 1), :] = xp[y : y + 1] if last else none
        if isinstance(i, int):
            planes = (inv, half, jnp.where(row == 0, ym, 0.0), jnp.where(row == dy - 1, yp, 0.0))
            for k, value in enumerate(planes):
                if i == 0:
                    pack_send[1, k] = value
                else:
                    pack_top[k] = value
        for c in range(3):
            d0 = rhs[c, i] * inv
            u[0, c, i + 1] = d0
            y_send[0, 0, c, pl.ds(i, 1), :] = d0[dy - 1 : dy]
            y_send[0, 1, c, pl.ds(i, 1), :] = d0[0:1]
        return jnp.maximum(best, (2.0 * total + 2.5 * bulk) / diagonal)

    best = sweep(weight_plane, 0, 0, jnp.zeros((dy, dz), jnp.float32), 2)
    m_own[...] = jnp.broadcast_to(jnp.max(best, axis=0, keepdims=True), m_own.shape)

    def halo_wait(turn, slot):
        exchange_wait(h_copy(turn, slot))
        place_halo(turn, slot)

    def place_halo(turn, slot):
        for c in range(3):
            u[slot, c, 0] = recv[turn, 0, c]
            above[c] = recv[turn, 1, c]
        for c in range(3):
            for k in range(dy):
                u[slot, c, dx + 1, k : k + 1, :] = above[c, pl.ds(undo[k], 1), :]

    def apply_plane(i, slot, low, high):
        v = [u[slot, c, i + 1] for c in range(3)]
        coupled = hb[i] * (v[0] + v[1] + v[2])
        out = []
        for c in range(3):
            ym, yp = y_near(v[c], low(c, i), high(c, i))
            zm, zp = z_near(v[c])
            near = wx[i] * u[slot, c, i] + wx[i + 1] * u[slot, c, i + 2]
            near = near + wym[i] * ym + wyp[i] * yp + wzm[i] * zm + wzp[i] * zp
            out.append(dg[i] * v[c] + coupled - near)
        return v, out

    def recv_rows(turn):
        return (
            lambda c, i: recv[turn, 2, c, pl.ds(i, 1), :],
            lambda c, i: recv[turn, 3, c, pl.ds(i, 1), :],
        )

    def bcoef(k):
        return jnp.broadcast_to(coef[k : k + 1, :], (dy, dz))

    def ring_start(own, store, ssem, rsem, peer_of, count, mine):
        copies = []
        for k in range(1, count):
            copies.append(remote(own, store.at[k], ssem.at[k], rsem.at[k], peer_of(k)))
        for copy in copies:
            copy.start()
        return copies

    group_peer = lambda k: (b, lax.rem(g + k, ng))
    brick_peer = lambda k: (lax.rem(b + k, nb), g)

    m_copies = ring_start(m_own, m_all, m_ssem, m_rsem, group_peer, ng, g)
    halo_wait(0, 0)

    low, high = recv_rows(0)

    def first_plane(i, _):
        _, out = apply_plane(i, 0, low, high)
        inv = invd[i]
        for c in range(3):
            r[c, i] = out[c]
            q = out[c] * inv
            u[1, c, i + 1] = q
            y_send[1, 0, c, pl.ds(i, 1), :] = q[dy - 1 : dy]
            y_send[1, 1, c, pl.ds(i, 1), :] = q[0:1]
        return 0

    sweep(first_plane, 1, 1, 0, SWEEP)

    def p_copy(d):
        return remote(
            pack_send.at[d], pack_recv.at[d], p_ssem.at[d], p_rsem.at[d], peers[d]
        )

    for q in range(4):
        for k in range(dy):
            pack_send[0, q, k : k + 1, :] = pack_top[q, pl.ds(order[k], 1), :]
    top = m_own[...]
    for k, copy in enumerate(m_copies):
        copy.wait()
        top = jnp.maximum(top, m_all[k + 1])
    m2_own[...] = top
    m2_copies = ring_start(m2_own, m2_all, m2_ssem, m2_rsem, brick_peer, nb, b)
    exchange_start(p_copy)
    halo_wait(1, 1)
    for k, copy in enumerate(m2_copies):
        copy.wait()
        top = jnp.maximum(top, m2_all[k + 1])
    upper = BOUND_MARGIN * jnp.broadcast_to(jnp.max(top, axis=1, keepdims=True), top.shape)
    lower = LOW_RATIO * upper
    theta = 0.5 * (upper + lower)
    delta = 0.5 * (upper - lower)
    sigma = theta / delta
    damping = 1.0 / sigma
    inv_theta = 1.0 / theta
    coef[0:8] = inv_theta
    rows = []
    for turn in range(1, CHEB):
        following = 1.0 / (2.0 * sigma - damping)
        rows.append((following * damping, 2.0 * following / delta))
        damping = following
    for turn, (a, c2) in enumerate(rows):
        coef[8 + 2 * turn : 9 + 2 * turn] = a[0:1]
        coef[9 + 2 * turn : 10 + 2 * turn] = c2[0:1]
    coef[14:15] = (rows[0][0] * inv_theta + rows[0][1])[0:1]
    coef[15:16] = (rows[0][1] * inv_theta)[0:1]

    alpha, beta, it = bcoef(14), bcoef(15), bcoef(0)

    def combine_plane(i, _):
        for c in range(3):
            d0 = u[0, c, i + 1]
            sol[c, i] = d0 * it
            res[c, i] = rhs[c, i] - r[c, i] * it
            u[0, c, i + 1] = alpha * d0 - beta * u[1, c, i + 1]
        return 0

    lax.fori_loop(0, dx, combine_plane, 0, unroll=UNROLL)
    for c in range(3):
        for p in (0, dx + 1):
            u[0, c, p] = alpha * u[0, c, p] - beta * u[1, c, p]
        for d in (2, 3):
            recv[1, d, c] = alpha[:dx] * recv[0, d, c] - beta[:dx] * recv[1, d, c]

    def step(slot, low, high, a, c2, following, summed=False, send=True):
        other = 1 - slot

        def plane(i, sums):
            v, out = apply_plane(i, slot, low, high)
            inv = invd[i]
            new = []
            for c in range(3):
                rest = res[c, i] - out[c]
                res[c, i] = rest
                sol[c, i] = sol[c, i] + v[c]
                if summed:
                    new.append(sums[c] + rest)
                if following is None:
                    continue
                ahead = c2 * (rest * inv)
                if a is not None:
                    ahead = ahead + a * v[c]
                u[other, c, i + 1] = ahead
                if not send:
                    continue
                y_send[following, 0, c, pl.ds(i, 1), :] = ahead[dy - 1 : dy]
                y_send[following, 1, c, pl.ds(i, 1), :] = ahead[0:1]
            return tuple(new)

        init = ()
        if summed:
            init = tuple(jnp.zeros((dy, dz), jnp.float32) for _ in range(3))
        return sweep(plane, following if send else None, other, init, SWEEP)

    def i_copy(d):
        return remote(inverse, inv_recv.at[d], i_ssem.at[d], i_rsem.at[d], peers[d])

    slot = 0
    for turn in range(1, CHEB):
        low, high = recv_rows(turn)
        if turn + 1 < CHEB:
            step(slot, low, high, bcoef(8 + 2 * turn), bcoef(9 + 2 * turn), turn + 1)
            slot = 1 - slot
            if turn == 1:
                exchange_start(i_copy, (0, 1))
            halo_wait(turn + 1, slot)
        else:
            sums = step(slot, low, high, None, bcoef(0), CHEB, summed=True)

    c_own[...] = jnp.zeros(c_own.shape, jnp.float32)
    for c in range(3):
        c_own[c : c + 1, :] = jnp.sum(sums[c], axis=0, keepdims=True)
    c_all[1, g] = c_own[...]

    def c_copy(q, k):
        slot = q * ng + k
        return remote(
            c_own, c_all.at[q, g], c_ssem.at[slot], c_rsem.at[slot],
            (b + 1 - q, lax.rem(g + k, ng)),
        )

    def c_arrival(q, k):
        slot = q * ng + k
        source = lax.rem(g + ng - k, ng)
        return remote(
            c_own, c_all.at[q, source], c_ssem.at[slot], c_rsem.at[slot],
            (b + 1 - q, lax.rem(g + k, ng)),
        )

    def coarse_all(to_do, flags):
        for q in (0, 2, 1):
            first = 1 if q == 1 else 0
            if q == 1:
                for k in range(first, ng):
                    to_do(q, k)
                continue

            @pl.when(flags[q])
            def _():
                for k in range(first, ng):
                    to_do(q, k)

    coarse_all(lambda q, k: c_copy(q, k).start(), {0: has[1], 2: has[0]})
    f_all[...] = jnp.zeros(f_all.shape, jnp.float32)
    exchange_wait(p_copy)
    exchange_wait(i_copy, (0, 1))
    coarse_all(lambda q, k: c_arrival(q, k).wait_recv(), {0: has[0], 2: has[1]})
    coarse_all(lambda q, k: c_copy(q, k).wait_send(), {0: has[1], 2: has[0]})

    cells_z = dz // BLOCK_Z
    size = 3 * cells_z * ng
    flat = c_all[...].reshape(3 * ng * 8, dz)
    li = lax.broadcasted_iota(jnp.int32, (dz, size), 0)
    ki = lax.broadcasted_iota(jnp.int32, (dz, size), 1)
    gather = jnp.where(li // BLOCK_Z == ki % cells_z, 1.0 / (dx * dy * BLOCK_Z), 0.0)
    spread = jnp.dot(flat, gather, precision=HIGHEST, preferred_element_type=jnp.float32)
    ri = lax.broadcasted_iota(jnp.int32, (ng * 8, size), 0)
    kk = lax.broadcasted_iota(jnp.int32, (ng * 8, size), 1) // cells_z
    mine = (ri // 8 == kk // 3) & (ri % 8 == kk % 3)
    bi = lax.broadcasted_iota(jnp.int32, (size, dz), 0)
    bl = lax.broadcasted_iota(jnp.int32, (size, dz), 1)
    placed = bi % cells_z == bl // BLOCK_Z
    for q in range(3):
        part = spread[q * ng * 8 : (q + 1) * ng * 8]
        vector = jnp.sum(jnp.where(mine, part, 0.0), axis=0, keepdims=True)
        matrix = inverse[...] if q == 1 else inv_recv[q // 2]
        correction = jnp.sum(matrix * vector, axis=1, keepdims=True)
        table = jnp.where(placed, jnp.broadcast_to(correction, (size, dz)), 0.0)
        for k in range(ng):
            for c in range(3):
                start = (k * 3 + c) * cells_z
                f_all[q, k + 1, c : c + 1, :] = jnp.sum(
                    table[start : start + cells_z], axis=0, keepdims=True
                )

    def full(q, at, c):
        return jnp.broadcast_to(f_all[q, at, c : c + 1, :], (dy, dz))

    own_fine = [full(1, g + 1, c) for c in range(3)]

    def fill_plane(i, _):
        for c in range(3):
            u[0, c, i + 1] = own_fine[c]
        return 0

    lax.fori_loop(0, dx, fill_plane, 0, unroll=UNROLL)
    for c in range(3):
        u[0, c, 0] = full(0, g + 1, c)
        u[0, c, dx + 1] = full(2, g + 1, c)
    it = bcoef(0)
    exchange_wait(h_copy(CHEB, 1))
    step(
        0,
        lambda c, i: f_all[1, g, c : c + 1, :],
        lambda c, i: f_all[1, g + 2, c : c + 1, :],
        None,
        it,
        CHEB,
        send=False,
    )

    def fine_on_face(d, near, cross, here, before, after):
        inv, half, w_low, w_high = [pack_recv[d, k] for k in range(4)]
        zm, zp = z_near(near)
        zm = jnp.where(lane == 0, 0.0, 0.5 * (near + zm))
        zp = jnp.where(lane == dz - 1, 0.0, 0.5 * (near + zp))
        rim = jnp.where((lane == 0) | (lane == dz - 1), near, 0.0)
        weight = 2.0 * half + cross + w_low + w_high + zm + zp + rim
        values = [full(*here, c) for c in range(3)]
        coupled = half * (values[0] + values[1] + values[2])
        for c in range(3):
            fm, fp = z_near(values[c])
            applied = weight * values[c] + coupled - cross * own_fine[c]
            applied = applied - zm * fm - zp * fp
            applied = applied - w_low * full(*before, c) - w_high * full(*after, c)
            recv[CHEB, d, c] = recv[CHEB, d, c] - it * (inv * applied)

    fine_on_face(0, s_recv[0], wx[0], (0, g + 1), (0, g), (0, g + 2))
    fine_on_face(1, s_recv[1], 0.5 * (s_recv[1] + s_send_up[...]), (2, g + 1), (2, g), (2, g + 2))
    fine_on_face(2, s_recv[2], 0.5 * (s_recv[2] + s_send_y[1]), (1, g), (0, g), (2, g))
    fine_on_face(3, s_recv[3], 0.5 * (s_recv[3] + s_send_y[0]), (1, g + 2), (0, g + 2), (2, g + 2))
    place_halo(CHEB, 1)

    slot = 1
    for turn in range(CHEB):
        if turn > 0:
            halo_wait(CHEB + turn, slot)
        low, high = recv_rows(CHEB + turn)
        if turn + 1 < CHEB:
            step(slot, low, high, bcoef(8 + 2 * turn), bcoef(9 + 2 * turn), CHEB + turn + 1)
            slot = 1 - slot
        else:
            step(slot, low, high, None, None, None)


def per_device(rhs, material, level, mortar, mu, lam, inverse):
    nb = lax.axis_size("bricks")
    ng = lax.axis_size("group")
    dx, dy, dz = material.shape
    f32 = jnp.float32
    vmem = pl.BlockSpec(memory_space=pltpu.VMEM)
    smem = pl.BlockSpec(memory_space=pltpu.SMEM)
    hbm = pl.BlockSpec(memory_space=pltpu.HBM)
    dma = pltpu.SemaphoreType.DMA
    grid = pltpu.VMEM((dx, dy, dz), f32)
    cg = inverse.shape[1]
    scratch = [
        pltpu.VMEM((3, dx, dy, dz), f32),
        pltpu.VMEM((dx, dy, dz), jnp.int32),
        pltpu.VMEM((cg, cg), f32),
        pltpu.VMEM((2, 3, dx + 2, dy, dz), f32),
        pltpu.VMEM((3, dx, dy, dz), f32),
        pltpu.VMEM((dx + 2, dy, dz), f32),
        pltpu.VMEM((dx + 1, dy, dz), f32),
        grid, grid, grid, grid, grid, grid, grid,
        pltpu.VMEM((16, dz), f32),
        pltpu.SMEM((dy,), jnp.int32),
        pltpu.VMEM((dy, dz), f32),
        pltpu.VMEM((2, dx, dz), f32),
        pltpu.VMEM((4, dx, dz), f32),
        pltpu.VMEM((3, dy, dz), f32),
        pltpu.VMEM((ROUNDS, 3, dy, dz), f32),
        pltpu.VMEM((ROUNDS, 2, 3, dx, dz), f32),
        pltpu.VMEM((ROUNDS, 4, 3, dx, dz), f32),
        pltpu.VMEM((8, dz), f32),
        pltpu.VMEM((ng, 8, dz), f32),
        pltpu.VMEM((8, dz), f32),
        pltpu.VMEM((nb, 8, dz), f32),
        pltpu.VMEM((8, dz), f32),
        pltpu.VMEM((3, ng, 8, dz), f32),
        pltpu.VMEM((3, ng + 2, 8, dz), f32),
        pltpu.VMEM((2, cg, cg), f32),
        pltpu.VMEM((4, 4, dx, dz), f32),
        pltpu.VMEM((4, dy, dz), f32),
        pltpu.VMEM((4, 4, dx, dz), f32),
        dma((3,)),
        dma((4,)), dma((4,)),
        dma((ROUNDS, 4)), dma((ROUNDS, 4)),
        dma((ng,)), dma((ng,)),
        dma((nb,)), dma((nb,)),
        dma((3 * ng,)), dma((3 * ng,)),
        dma((4,)), dma((4,)),
        dma((2,)), dma((2,)),
    ]
    rhs, material, inverse = (
        pltpu.with_memory_space_constraint(x, pltpu.HBM) for x in (rhs, material, inverse)
    )
    return pl.pallas_call(
        functools.partial(kernel, nb, ng, dx, dy, dz),
        out_shape=(
            jax.ShapeDtypeStruct(rhs.shape, f32),
            jax.ShapeDtypeStruct(rhs.shape, f32),
        ),
        in_specs=[hbm, hbm, vmem, smem, smem, smem, hbm],
        out_specs=(vmem, vmem),
        scratch_shapes=scratch,
        compiler_params=pltpu.CompilerParams(
            collective_id=0, has_side_effects=True, vmem_limit_bytes=16 * 2**20
        ),
    )(rhs, material, level, mortar, mu, lam, inverse)


def solution(mesh):
    return jax.shard_map(
        per_device,
        mesh=mesh,
        in_specs=(
            P(None, "bricks", "group", None),
            P("bricks", "group", None),
            P("bricks", "group"),
            P("bricks", "group", None),
            P(),
            P(),
            P("bricks", None, None),
        ),
        out_specs=(P(None, "bricks", "group", None), P(None, "bricks", "group", None)),
        check_vma=False,
    )
```

```python
import functools

import jax
import jax.numpy as jnp
from jax import lax
from jax.experimental import pallas as pl
from jax.experimental.pallas import tpu as pltpu
from jax.sharding import PartitionSpec as P

BLOCK_Z = 32
CHEB = 4
LOW_RATIO = 0.15
BOUND_MARGIN = 1.1
ROUNDS = 2 * CHEB
UNROLL = 4
SWEEP = 7
HIGHEST = lax.Precision.HIGHEST


def kernel(
    nb, ng, dx, dy, dz,
    rhs_in, material_in, level, mortar, mu, lam, inverse_in,
    sol, res, rhs, material, inverse,
    u, r, shear, wx, wyp, wym, wzp, wzm, dg, hb, invd, coef, undo,
    s_send_up, s_send_y, s_recv, above, up_send, y_send, recv,
    m_own, m_all, m2_own, m2_all, c_own, c_all, f_all, inv_recv, pack_send, pack_top, pack_recv, in_sem,
    s_ssem, s_rsem, h_ssem, h_rsem,
    m_ssem, m_rsem, m2_ssem, m2_rsem, c_ssem, c_rsem, p_ssem, p_rsem, i_ssem, i_rsem,
):
    b = lax.axis_index("bricks")
    g = lax.axis_index("group")
    has = [b > 0, b < nb - 1, g > 0, g < ng - 1]
    sends = [has[1], has[0], has[3], has[2]]
    peers = [(b + 1, g), (b - 1, g), (b, g + 1), (b, g - 1)]

    def remote(src, dst, ssem, rsem, peer):
        return pltpu.make_async_remote_copy(
            src_ref=src, dst_ref=dst, send_sem=ssem, recv_sem=rsem,
            device_id=peer, device_id_type=pl.DeviceIdType.MESH,
        )

    barrier = pltpu.get_barrier_semaphore()
    others = [(b, lax.rem(g + k, ng)) for k in range(1, ng)]
    others += [(lax.rem(b + k, nb), g) for k in range(1, nb)]
    around = [(lax.rem(g + k, ng)) for k in range(1, ng)]
    for peer in others:
        pl.semaphore_signal(
            barrier, inc=1, device_id=peer, device_id_type=pl.DeviceIdType.MESH
        )
    for d in range(2):
        @pl.when(has[d])
        def _():
            for at in around:
                pl.semaphore_signal(
                    barrier, inc=1, device_id=(b - 1 + 2 * d, at),
                    device_id_type=pl.DeviceIdType.MESH,
                )

    def fetch(k):
        source = [material_in, rhs_in, inverse_in.at[0]][k]
        return pltpu.make_async_copy(source, [material, rhs, inverse][k], in_sem.at[k])

    for k in range(3):
        fetch(k).start()

    grade = jnp.broadcast_to(level[...], (dy, dz))
    scale = jnp.where(grade == 0, 1.0, jnp.where(grade == 1, 4.0, 16.0))
    zero_face = jnp.zeros((3, dx, dz), jnp.float32)

    order = [mortar[0, 0, k] for k in range(dy)]
    for k in range(dy):
        total = jnp.int32(0)
        for j in range(dy):
            total = jnp.where(order[j] == k, jnp.int32(j), total)
        undo[k] = total

    def lookup(ids, table):
        total = jnp.where(ids == 0, table[0], 0.0)
        for entry in range(1, 4):
            total = jnp.where(ids == entry, table[entry], total)
        return total * scale

    def shear_plane(i, _):
        ids = material[i]
        plane = lookup(ids, mu)
        shear[i + 1] = plane
        hb[i] = lookup(ids, lam)
        s_send_y[0, pl.ds(i, 1), :] = plane[dy - 1 : dy]
        s_send_y[1, pl.ds(i, 1), :] = plane[0:1]
        return 0

    fetch(0).wait()
    lax.fori_loop(0, dx, shear_plane, 0, unroll=UNROLL)
    for k in range(dy):
        s_send_up[k : k + 1, :] = shear[dx, pl.ds(order[k], 1), :]

    both = jnp.where(has[0], len(around), 0) + jnp.where(has[1], len(around), 0)
    pl.semaphore_wait(barrier, len(others) + both)

    def s_copy(d):
        src = [s_send_up, shear.at[1], s_send_y.at[0], s_send_y.at[1]][d]
        return remote(src, s_recv.at[d], s_ssem.at[d], s_rsem.at[d], peers[d])

    def exchange_start(copy, directions=(0, 1, 2, 3)):
        for d in directions:
            @pl.when(sends[d])
            def _():
                copy(d).start()

    def exchange_wait(copy, directions=(0, 1, 2, 3)):
        for d in directions:
            @pl.when(has[d])
            def _():
                copy(d).wait_recv()
        for d in directions:
            @pl.when(sends[d])
            def _():
                copy(d).wait_send()

    exchange_start(s_copy)

    @pl.when(b == 0)
    def _():
        s_recv[0] = shear[1]

    @pl.when(b == nb - 1)
    def _():
        shear[dx + 1] = shear[dx]
        s_recv[1] = shear[dx]

    @pl.when(g == 0)
    def _():
        s_recv[2] = s_send_y[1]

    @pl.when(g == ng - 1)
    def _():
        s_recv[3] = s_send_y[0]

    for d in range(4):
        @pl.when(jnp.logical_not(has[d]))
        def _():
            for turn in range(ROUNDS):
                recv[turn, d] = zero_face
            pack_recv[d] = jnp.zeros(pack_recv.shape[1:], jnp.float32)
            if d < 2:
                inv_recv[d] = jnp.zeros(inv_recv.shape[1:], jnp.float32)
                c_all[2 * d] = jnp.zeros(c_all.shape[1:], jnp.float32)

    fetch(1).wait()
    fetch(2).wait()
    exchange_wait(s_copy)
    shear[0] = s_recv[0]

    @pl.when(b < nb - 1)
    def _():
        for k in range(dy):
            shear[dx + 1, k : k + 1, :] = s_recv[1, pl.ds(undo[k], 1), :]

    row = lax.broadcasted_iota(jnp.int32, (dy, dz), 0)
    lane = lax.broadcasted_iota(jnp.int32, (dy, dz), 1)

    def y_near(v, low, high):
        ym = jnp.where(row == 0, jnp.broadcast_to(low, v.shape), pltpu.roll(v, 1, 0))
        yp = jnp.where(
            row == dy - 1, jnp.broadcast_to(high, v.shape), pltpu.roll(v, dy - 1, 0)
        )
        return ym, yp

    def z_near(v):
        return pltpu.roll(v, 1, 1), pltpu.roll(v, dz - 1, 1)

    def h_copy(turn, slot):
        def copy(d):
            src = [
                up_send.at[turn], u.at[slot, :, 1], y_send.at[turn, 0], y_send.at[turn, 1]
            ][d]
            return remote(
                src, recv.at[turn, d], h_ssem.at[turn, d], h_rsem.at[turn, d], peers[d]
            )
        return copy

    even = lax.rem(b, 2) == 0

    def sweep(plane, turn, slot, carry, unroll, arrive=None):
        if arrive is not None:
            carry = lax.fori_loop(1, dx - 1, plane, carry, unroll=unroll)
            arrive()
        carry = plane(0, carry)
        carry = plane(dx - 1, carry)
        if turn is not None:
            copy = h_copy(turn, slot)

            @pl.when(sends[1] & even)
            def _():
                copy(1).start()

            for c in range(3):
                for k in range(dy):
                    up_send[turn, c, k : k + 1, :] = u[slot, c, dx, pl.ds(order[k], 1), :]
            exchange_start(copy, (0,))

            @pl.when(sends[1] & jnp.logical_not(even))
            def _():
                copy(1).start()

        if arrive is None:
            carry = lax.fori_loop(1, dx - 1, plane, carry, unroll=unroll)
        if turn is not None:
            exchange_start(h_copy(turn, slot), (2, 3))
        return carry

    wx[0] = 0.5 * (shear[0] + shear[1])
    wx[dx] = 0.5 * (shear[dx] + shear[dx + 1])

    def weight_plane(i, best):
        s = shear[i + 1]
        xp = 0.5 * (s + shear[i + 2])
        wx[i + 1] = xp
        xm = 0.5 * (s + shear[i])
        ym, yp = y_near(s, s_recv[2, pl.ds(i, 1), :], s_recv[3, pl.ds(i, 1), :])
        ym = 0.5 * (s + ym)
        yp = 0.5 * (s + yp)
        zm, zp = z_near(s)
        zm = 0.5 * (s + zm)
        zp = 0.5 * (s + zp)
        wyp[i] = yp
        wym[i] = ym
        wzp[i] = jnp.where(lane == dz - 1, 0.0, zp)
        wzm[i] = jnp.where(lane == 0, 0.0, zm)
        total = xp + xm + yp + ym + jnp.where(lane == dz - 1, s, zp) + jnp.where(lane == 0, s, zm)
        bulk = hb[i]
        diagonal = total + 1.5 * bulk
        inv = 1.0 / diagonal
        invd[i] = inv
        dg[i] = total + bulk
        half = 0.5 * bulk
        hb[i] = half
        none = jnp.zeros((1, dz), jnp.float32)
        for d, y in ((2, dy - 1), (3, 0)):
            pack_send[d, 0, pl.ds(i, 1), :] = inv[y : y + 1]
            pack_send[d, 1, pl.ds(i, 1), :] = half[y : y + 1]
            first, last = isinstance(i, int) and i == 0, isinstance(i, int) and i == dx - 1
            pack_send[d, 2, pl.ds(i, 1), :] = xm[y : y + 1] if first else none
            pack_send[d, 3, pl.ds(i, 1), :] = xp[y : y + 1] if last else none
        if isinstance(i, int):
            planes = (inv, half, jnp.where(row == 0, ym, 0.0), jnp.where(row == dy - 1, yp, 0.0))
            for k, value in enumerate(planes):
                if i == 0:
                    pack_send[1, k] = value
                else:
                    pack_top[k] = value
        for c in range(3):
            d0 = rhs[c, i] * inv
            u[0, c, i + 1] = d0
            y_send[0, 0, c, pl.ds(i, 1), :] = d0[dy - 1 : dy]
            y_send[0, 1, c, pl.ds(i, 1), :] = d0[0:1]
        return jnp.maximum(best, (2.0 * total + 2.5 * bulk) / diagonal)

    best = sweep(weight_plane, 0, 0, jnp.zeros((dy, dz), jnp.float32), 2)
    m_own[...] = jnp.broadcast_to(jnp.max(best, axis=0, keepdims=True), m_own.shape)

    def halo_wait(turn, slot):
        exchange_wait(h_copy(turn, slot))
        place_halo(turn, slot)

    def x_arrival(turn, slot):
        def arrive():
            exchange_wait(h_copy(turn, slot), (0, 1))
            place_halo(turn, slot)
        return arrive

    def place_halo(turn, slot):
        for c in range(3):
            u[slot, c, 0] = recv[turn, 0, c]
            above[c] = recv[turn, 1, c]
        for c in range(3):
            for k in range(dy):
                u[slot, c, dx + 1, k : k + 1, :] = above[c, pl.ds(undo[k], 1), :]

    def apply_plane(i, slot, low, high):
        v = [u[slot, c, i + 1] for c in range(3)]
        coupled = hb[i] * (v[0] + v[1] + v[2])
        out = []
        for c in range(3):
            ym, yp = y_near(v[c], low(c, i), high(c, i))
            zm, zp = z_near(v[c])
            near = wx[i] * u[slot, c, i] + wx[i + 1] * u[slot, c, i + 2]
            near = near + wym[i] * ym + wyp[i] * yp + wzm[i] * zm + wzp[i] * zp
            out.append(dg[i] * v[c] + coupled - near)
        return v, out

    def recv_rows(turn):
        return (
            lambda c, i: recv[turn, 2, c, pl.ds(i, 1), :],
            lambda c, i: recv[turn, 3, c, pl.ds(i, 1), :],
        )

    def bcoef(k):
        return jnp.broadcast_to(coef[k : k + 1, :], (dy, dz))

    def ring_start(own, store, ssem, rsem, peer_of, count, mine):
        copies = []
        for k in range(1, count):
            copies.append(remote(own, store.at[k], ssem.at[k], rsem.at[k], peer_of(k)))
        for copy in copies:
            copy.start()
        return copies

    group_peer = lambda k: (b, lax.rem(g + k, ng))
    brick_peer = lambda k: (lax.rem(b + k, nb), g)

    m_copies = ring_start(m_own, m_all, m_ssem, m_rsem, group_peer, ng, g)
    halo_wait(0, 0)

    low, high = recv_rows(0)

    def first_plane(i, _):
        _, out = apply_plane(i, 0, low, high)
        inv = invd[i]
        for c in range(3):
            r[c, i] = out[c]
            q = out[c] * inv
            u[1, c, i + 1] = q
            y_send[1, 0, c, pl.ds(i, 1), :] = q[dy - 1 : dy]
            y_send[1, 1, c, pl.ds(i, 1), :] = q[0:1]
        return 0

    sweep(first_plane, 1, 1, 0, SWEEP)

    def p_copy(d):
        return remote(
            pack_send.at[d], pack_recv.at[d], p_ssem.at[d], p_rsem.at[d], peers[d]
        )

    for q in range(4):
        for k in range(dy):
            pack_send[0, q, k : k + 1, :] = pack_top[q, pl.ds(order[k], 1), :]
    top = m_own[...]
    for k, copy in enumerate(m_copies):
        copy.wait()
        top = jnp.maximum(top, m_all[k + 1])
    m2_own[...] = top
    m2_copies = ring_start(m2_own, m2_all, m2_ssem, m2_rsem, brick_peer, nb, b)
    exchange_start(p_copy)
    halo_wait(1, 1)
    for k, copy in enumerate(m2_copies):
        copy.wait()
        top = jnp.maximum(top, m2_all[k + 1])
    upper = BOUND_MARGIN * jnp.broadcast_to(jnp.max(top, axis=1, keepdims=True), top.shape)
    lower = LOW_RATIO * upper
    theta = 0.5 * (upper + lower)
    delta = 0.5 * (upper - lower)
    sigma = theta / delta
    damping = 1.0 / sigma
    inv_theta = 1.0 / theta
    coef[0:8] = inv_theta
    rows = []
    for turn in range(1, CHEB):
        following = 1.0 / (2.0 * sigma - damping)
        rows.append((following * damping, 2.0 * following / delta))
        damping = following
    for turn, (a, c2) in enumerate(rows):
        coef[8 + 2 * turn : 9 + 2 * turn] = a[0:1]
        coef[9 + 2 * turn : 10 + 2 * turn] = c2[0:1]
    coef[14:15] = (rows[0][0] * inv_theta + rows[0][1])[0:1]
    coef[15:16] = (rows[0][1] * inv_theta)[0:1]

    alpha, beta, it = bcoef(14), bcoef(15), bcoef(0)

    def combine_plane(i, _):
        for c in range(3):
            d0 = u[0, c, i + 1]
            sol[c, i] = d0 * it
            res[c, i] = rhs[c, i] - r[c, i] * it
            u[0, c, i + 1] = alpha * d0 - beta * u[1, c, i + 1]
        return 0

    lax.fori_loop(0, dx, combine_plane, 0, unroll=UNROLL)
    for c in range(3):
        for p in (0, dx + 1):
            u[0, c, p] = alpha * u[0, c, p] - beta * u[1, c, p]
        for d in (2, 3):
            recv[1, d, c] = alpha[:dx] * recv[0, d, c] - beta[:dx] * recv[1, d, c]

    def step(slot, low, high, a, c2, following, summed=False, send=True, arrive=None):
        other = 1 - slot

        def plane(i, sums):
            v, out = apply_plane(i, slot, low, high)
            inv = invd[i]
            new = []
            for c in range(3):
                rest = res[c, i] - out[c]
                res[c, i] = rest
                sol[c, i] = sol[c, i] + v[c]
                if summed:
                    new.append(sums[c] + rest)
                if following is None:
                    continue
                ahead = c2 * (rest * inv)
                if a is not None:
                    ahead = ahead + a * v[c]
                u[other, c, i + 1] = ahead
                if not send:
                    continue
                y_send[following, 0, c, pl.ds(i, 1), :] = ahead[dy - 1 : dy]
                y_send[following, 1, c, pl.ds(i, 1), :] = ahead[0:1]
            return tuple(new)

        init = ()
        if summed:
            init = tuple(jnp.zeros((dy, dz), jnp.float32) for _ in range(3))
        return sweep(plane, following if send else None, other, init, SWEEP, arrive)

    def i_copy(d):
        return remote(inverse, inv_recv.at[d], i_ssem.at[d], i_rsem.at[d], peers[d])

    slot = 0
    for turn in range(1, CHEB):
        low, high = recv_rows(turn)
        if turn + 1 < CHEB:
            step(slot, low, high, bcoef(8 + 2 * turn), bcoef(9 + 2 * turn), turn + 1)
            slot = 1 - slot
            if turn == 1:
                exchange_start(i_copy, (0, 1))
            if turn + 2 < CHEB:
                halo_wait(turn + 1, slot)
            else:
                exchange_wait(h_copy(turn + 1, slot), (2, 3))
        else:
            sums = step(
                slot, low, high, None, bcoef(0), CHEB, summed=True, arrive=x_arrival(turn, slot)
            )

    c_own[...] = jnp.zeros(c_own.shape, jnp.float32)
    for c in range(3):
        c_own[c : c + 1, :] = jnp.sum(sums[c], axis=0, keepdims=True)
    c_all[1, g] = c_own[...]

    def c_copy(q, k):
        slot = q * ng + k
        return remote(
            c_own, c_all.at[q, g], c_ssem.at[slot], c_rsem.at[slot],
            (b + 1 - q, lax.rem(g + k, ng)),
        )

    def c_arrival(q, k):
        slot = q * ng + k
        source = lax.rem(g + ng - k, ng)
        return remote(
            c_own, c_all.at[q, source], c_ssem.at[slot], c_rsem.at[slot],
            (b + 1 - q, lax.rem(g + k, ng)),
        )

    def coarse_all(to_do, flags):
        for q in (0, 2, 1):
            first = 1 if q == 1 else 0
            if q == 1:
                for k in range(first, ng):
                    to_do(q, k)
                continue

            @pl.when(flags[q])
            def _():
                for k in range(first, ng):
                    to_do(q, k)

    coarse_all(lambda q, k: c_copy(q, k).start(), {0: has[1], 2: has[0]})
    f_all[...] = jnp.zeros(f_all.shape, jnp.float32)
    exchange_wait(p_copy)
    exchange_wait(i_copy, (0, 1))
    coarse_all(lambda q, k: c_arrival(q, k).wait_recv(), {0: has[0], 2: has[1]})
    coarse_all(lambda q, k: c_copy(q, k).wait_send(), {0: has[1], 2: has[0]})

    cells_z = dz // BLOCK_Z
    size = 3 * cells_z * ng
    flat = c_all[...].reshape(3 * ng * 8, dz)
    li = lax.broadcasted_iota(jnp.int32, (dz, size), 0)
    ki = lax.broadcasted_iota(jnp.int32, (dz, size), 1)
    gather = jnp.where(li // BLOCK_Z == ki % cells_z, 1.0 / (dx * dy * BLOCK_Z), 0.0)
    spread = jnp.dot(flat, gather, precision=HIGHEST, preferred_element_type=jnp.float32)
    ri = lax.broadcasted_iota(jnp.int32, (ng * 8, size), 0)
    kk = lax.broadcasted_iota(jnp.int32, (ng * 8, size), 1) // cells_z
    mine = (ri // 8 == kk // 3) & (ri % 8 == kk % 3)
    bi = lax.broadcasted_iota(jnp.int32, (size, dz), 0)
    bl = lax.broadcasted_iota(jnp.int32, (size, dz), 1)
    placed = bi % cells_z == bl // BLOCK_Z
    for q in range(3):
        part = spread[q * ng * 8 : (q + 1) * ng * 8]
        vector = jnp.sum(jnp.where(mine, part, 0.0), axis=0, keepdims=True)
        matrix = inverse[...] if q == 1 else inv_recv[q // 2]
        correction = jnp.sum(matrix * vector, axis=1, keepdims=True)
        table = jnp.where(placed, jnp.broadcast_to(correction, (size, dz)), 0.0)
        for k in range(ng):
            for c in range(3):
                start = (k * 3 + c) * cells_z
                f_all[q, k + 1, c : c + 1, :] = jnp.sum(
                    table[start : start + cells_z], axis=0, keepdims=True
                )

    def full(q, at, c):
        return jnp.broadcast_to(f_all[q, at, c : c + 1, :], (dy, dz))

    own_fine = [full(1, g + 1, c) for c in range(3)]

    def fill_plane(i, _):
        for c in range(3):
            u[0, c, i + 1] = own_fine[c]
        return 0

    lax.fori_loop(0, dx, fill_plane, 0, unroll=UNROLL)
    for c in range(3):
        u[0, c, 0] = full(0, g + 1, c)
        u[0, c, dx + 1] = full(2, g + 1, c)
    it = bcoef(0)
    exchange_wait(h_copy(CHEB, 1))
    step(
        0,
        lambda c, i: f_all[1, g, c : c + 1, :],
        lambda c, i: f_all[1, g + 2, c : c + 1, :],
        None,
        it,
        CHEB,
        send=False,
    )

    def fine_on_face(d, near, cross, here, before, after):
        inv, half, w_low, w_high = [pack_recv[d, k] for k in range(4)]
        zm, zp = z_near(near)
        zm = jnp.where(lane == 0, 0.0, 0.5 * (near + zm))
        zp = jnp.where(lane == dz - 1, 0.0, 0.5 * (near + zp))
        rim = jnp.where((lane == 0) | (lane == dz - 1), near, 0.0)
        weight = 2.0 * half + cross + w_low + w_high + zm + zp + rim
        values = [full(*here, c) for c in range(3)]
        coupled = half * (values[0] + values[1] + values[2])
        for c in range(3):
            fm, fp = z_near(values[c])
            applied = weight * values[c] + coupled - cross * own_fine[c]
            applied = applied - zm * fm - zp * fp
            applied = applied - w_low * full(*before, c) - w_high * full(*after, c)
            recv[CHEB, d, c] = recv[CHEB, d, c] - it * (inv * applied)

    fine_on_face(0, s_recv[0], wx[0], (0, g + 1), (0, g), (0, g + 2))
    fine_on_face(1, s_recv[1], 0.5 * (s_recv[1] + s_send_up[...]), (2, g + 1), (2, g), (2, g + 2))
    fine_on_face(2, s_recv[2], 0.5 * (s_recv[2] + s_send_y[1]), (1, g), (0, g), (2, g))
    fine_on_face(3, s_recv[3], 0.5 * (s_recv[3] + s_send_y[0]), (1, g + 2), (0, g + 2), (2, g + 2))
    place_halo(CHEB, 1)

    slot = 1
    for turn in range(CHEB):
        if turn + 1 == CHEB:
            exchange_wait(h_copy(CHEB + turn, slot), (2, 3))
        elif turn > 0:
            halo_wait(CHEB + turn, slot)
        low, high = recv_rows(CHEB + turn)
        if turn + 1 < CHEB:
            step(slot, low, high, bcoef(8 + 2 * turn), bcoef(9 + 2 * turn), CHEB + turn + 1)
            slot = 1 - slot
        else:
            step(
                slot, low, high, None, None, None, arrive=x_arrival(CHEB + turn, slot)
            )


def per_device(rhs, material, level, mortar, mu, lam, inverse):
    nb = lax.axis_size("bricks")
    ng = lax.axis_size("group")
    dx, dy, dz = material.shape
    f32 = jnp.float32
    vmem = pl.BlockSpec(memory_space=pltpu.VMEM)
    smem = pl.BlockSpec(memory_space=pltpu.SMEM)
    hbm = pl.BlockSpec(memory_space=pltpu.HBM)
    dma = pltpu.SemaphoreType.DMA
    grid = pltpu.VMEM((dx, dy, dz), f32)
    cg = inverse.shape[1]
    scratch = [
        pltpu.VMEM((3, dx, dy, dz), f32),
        pltpu.VMEM((dx, dy, dz), jnp.int32),
        pltpu.VMEM((cg, cg), f32),
        pltpu.VMEM((2, 3, dx + 2, dy, dz), f32),
        pltpu.VMEM((3, dx, dy, dz), f32),
        pltpu.VMEM((dx + 2, dy, dz), f32),
        pltpu.VMEM((dx + 1, dy, dz), f32),
        grid, grid, grid, grid, grid, grid, grid,
        pltpu.VMEM((16, dz), f32),
        pltpu.SMEM((dy,), jnp.int32),
        pltpu.VMEM((dy, dz), f32),
        pltpu.VMEM((2, dx, dz), f32),
        pltpu.VMEM((4, dx, dz), f32),
        pltpu.VMEM((3, dy, dz), f32),
        pltpu.VMEM((ROUNDS, 3, dy, dz), f32),
        pltpu.VMEM((ROUNDS, 2, 3, dx, dz), f32),
        pltpu.VMEM((ROUNDS, 4, 3, dx, dz), f32),
        pltpu.VMEM((8, dz), f32),
        pltpu.VMEM((ng, 8, dz), f32),
        pltpu.VMEM((8, dz), f32),
        pltpu.VMEM((nb, 8, dz), f32),
        pltpu.VMEM((8, dz), f32),
        pltpu.VMEM((3, ng, 8, dz), f32),
        pltpu.VMEM((3, ng + 2, 8, dz), f32),
        pltpu.VMEM((2, cg, cg), f32),
        pltpu.VMEM((4, 4, dx, dz), f32),
        pltpu.VMEM((4, dy, dz), f32),
        pltpu.VMEM((4, 4, dx, dz), f32),
        dma((3,)),
        dma((4,)), dma((4,)),
        dma((ROUNDS, 4)), dma((ROUNDS, 4)),
        dma((ng,)), dma((ng,)),
        dma((nb,)), dma((nb,)),
        dma((3 * ng,)), dma((3 * ng,)),
        dma((4,)), dma((4,)),
        dma((2,)), dma((2,)),
    ]
    rhs, material, inverse, mortar, mu, lam = (
        pltpu.with_memory_space_constraint(x, pltpu.HBM)
        for x in (rhs, material, inverse, mortar, mu, lam)
    )
    return pl.pallas_call(
        functools.partial(kernel, nb, ng, dx, dy, dz),
        out_shape=(
            jax.ShapeDtypeStruct(rhs.shape, f32),
            jax.ShapeDtypeStruct(rhs.shape, f32),
        ),
        in_specs=[hbm, hbm, vmem, smem, smem, smem, hbm],
        out_specs=(vmem, vmem),
        scratch_shapes=scratch,
        compiler_params=pltpu.CompilerParams(
            collective_id=0, has_side_effects=True, vmem_limit_bytes=16 * 2**20
        ),
    )(rhs, material, level, mortar, mu, lam, inverse)


def solution(mesh):
    return jax.shard_map(
        per_device,
        mesh=mesh,
        in_specs=(
            P(None, "bricks", "group", None),
            P("bricks", "group", None),
            P("bricks", "group"),
            P("bricks", "group", None),
            P(),
            P(),
            P("bricks", None, None),
        ),
        out_specs=(P(None, "bricks", "group", None), P(None, "bricks", "group", None)),
        check_vma=False,
    )
```
